512 devices in a mesh: gx: 64 (over x, z_lo, y), gy: 8 (over z_hi, core).
Axes of the slice: x: 4, y: 8, z: 8 (z_hi: 4, z_lo: 2; z = z_hi * 2 + z_lo), core: 2. Of those that a mesh axis runs over, the one named last changes fastest.
Arguments:
- flow_field: bfloat16 [256, 128, 64, 128], P('gx', 'gy'), may hold values from -6 to 6
- spectral_weight: bfloat16 [512, 64, 2, 64, 128], P(('gy', 'gx')), may hold values from -1 to 1
- conv_weight: bfloat16 [3, 3, 3, 128, 128], replicated, may hold values from -0.109375 to 0.109375
- channel_bias: float32 [128], replicated, may hold values from -3 to 3
Outputs:
- activated: bfloat16 [256, 128, 64, 128], P('gx', 'gy')
The draws below stay inside these ranges and needn't reach their ends.
All inputs are finite; a program needn't handle non-finite values.
Results may differ from the reference program's by a relative error of at most 0.018.
Values may be sent and summed in bfloat16 or wider, within the bound.
A program may use at most 128 MiB of HBM per device.

```python
import math
import jax
import jax.numpy as jnp
from jax import lax

C = 128
MX = 64
MY = 16
MZ = 16
CZ = 64
NX = 256
NY = 128


def shard_levels(own_key, extent, shards, low, high):
    def one(dim, shards_of):
        steps = jax.random.uniform(jax.random.fold_in(jax.random.fold_in(own_key, 6), dim), (shards_of,), jnp.float32, low / len(shards), high / len(shards))
        return jnp.repeat(jnp.exp(steps), extent[dim] // shards_of).reshape((-1,) + (1,) * (len(extent) - dim - 1))

    factor_of = one(*shards[0])
    for cut in shards[1:]:
        factor_of = factor_of * one(*cut)
    return factor_of


def noise(stream_key, extent, spread, bound, split=(), kind=jnp.bfloat16):
    drawn = spread * jax.random.normal(stream_key, extent, jnp.float32)
    if split:
        drawn = drawn * shard_levels(stream_key, extent, split, -0.22, 0.18)
    return jnp.clip(drawn, -bound, bound).astype(kind)


def setup_inputs(seed: int = 0) -> dict:
    arg_keys = jax.random.split(jax.random.key(seed), 5)
    flow_field = noise(arg_keys[0], (NX, NY, CZ, C), 1.0, 6.0, ((0, 64), (1, 8)))
    spectral_weight = noise(arg_keys[1], (2 * MY * MZ, MX, 2, C // 2, C), (C // 4) ** -0.5, 1.0, ((0, 512),))
    conv_weight = noise(arg_keys[2], (3, 3, 3, C, C), (27 * C) ** -0.5, 0.109375)
    channel_bias = noise(arg_keys[3], (C,), 0.5, 3.0, (), jnp.float32)
    return {"flow_field": flow_field, "spectral_weight": spectral_weight, "conv_weight": conv_weight, "channel_bias": channel_bias}


def signed_modes(mode_count):
    position = jnp.arange(mode_count, dtype=jnp.int32)
    return jnp.where(position < mode_count // 2, position, position - mode_count)


def angle_grid(first, second, length):
    phase_turns = (first[:, None] * second[None, :]) % length
    return phase_turns.astype(jnp.float32) * (2.0 * math.pi / length)


def real_table(first, second, length, factor):
    angles = angle_grid(first, second, length)
    return jnp.stack([jnp.cos(angles) * factor, -jnp.sin(angles) * factor])


def complex_table(first, second, length, factor, direction):
    angles = angle_grid(first, second, length)
    cosine = jnp.cos(angles) * factor
    sine_part = jnp.sin(angles) * factor
    return jnp.stack([jnp.stack([cosine, direction * sine_part]), jnp.stack([-direction * sine_part, cosine])])


def reference(flow_field, spectral_weight, conv_weight, channel_bias):
    size_x, size_y, size_z, channels = flow_field.shape
    highest = lax.Precision.HIGHEST
    grid_x = jnp.arange(size_x, dtype=jnp.int32)
    grid_y = jnp.arange(size_y, dtype=jnp.int32)
    grid_z = jnp.arange(size_z, dtype=jnp.int32)
    modes_z = jnp.arange(MZ, dtype=jnp.int32)
    forward_z = real_table(grid_z, modes_z, size_z, size_z ** -0.5).astype(jnp.bfloat16).astype(jnp.float32)
    forward_y = complex_table(grid_y, signed_modes(MY), size_y, size_y ** -0.5, -1.0)
    forward_x = complex_table(grid_x, signed_modes(MX), size_x, size_x ** -0.5, -1.0)
    backward_x = complex_table(signed_modes(MX), grid_x, size_x, MX ** -0.5, 1.0)
    backward_y = complex_table(signed_modes(MY), grid_y, size_y, MY ** -0.5, 1.0)
    backward_z = real_table(modes_z, grid_z, size_z, MZ ** -0.5).astype(jnp.bfloat16).astype(jnp.float32)

    def plane_modes(plane):
        z_spectrum = jnp.einsum('yzc,pzk->pykc', plane.astype(jnp.float32), forward_z, precision=highest)
        return jnp.einsum('pykc,pqyj->qjkc', z_spectrum, forward_y, precision=highest)

    y_spectrum = lax.map(plane_modes, flow_field)
    x_spectrum = jnp.einsum('xpjkc,pqxm->qmjkc', y_spectrum, forward_x, precision=highest)
    x_input = x_spectrum.astype(jnp.bfloat16).astype(jnp.float32).reshape(2, MX, 2 * MY * MZ, channels // 2)
    products = jnp.einsum('pmjc,jmqco->pqmjo', x_input, spectral_weight.astype(jnp.float32), precision=highest)
    mixed_modes = jnp.stack([products[0, 0] - products[1, 1], products[0, 1] + products[1, 0]])
    mixed_modes = mixed_modes.reshape(2, MX, MY * MZ, 2, channels).sum(axis=3).reshape(2, MX, MY, MZ, channels)
    x_inverse = jnp.einsum('pmjkc,pqmx->xqjkc', mixed_modes, backward_x, precision=highest)
    padded = jnp.pad(flow_field, ((1, 1), (1, 1), (1, 1), (0, 0)))
    kernel = conv_weight.astype(jnp.float32).reshape(3, 3, 3 * channels, channels)

    def plane_out(pieces):
        coefficients, start = pieces
        y_inverse = jnp.einsum('pjkc,pqjy->qykc', coefficients, backward_y, precision=highest)
        y_inverse = y_inverse.astype(jnp.bfloat16).astype(jnp.float32)
        spectral = jnp.einsum('pykc,pkz->yzc', y_inverse, backward_z, precision=highest)
        slab = lax.dynamic_slice_in_dim(padded, start, 3, 0).astype(jnp.float32)
        stacked = jnp.concatenate([slab[:, :, 0:size_z], slab[:, :, 1:size_z + 1], slab[:, :, 2:size_z + 2]], axis=3)
        accumulated = jnp.zeros((size_y, size_z, channels), jnp.float32)
        for shift_x in range(3):
            for shift_y in range(3):
                accumulated = accumulated + jnp.dot(stacked[shift_x, shift_y:shift_y + size_y], kernel[shift_x, shift_y], precision=highest, preferred_element_type=jnp.float32)
        return jax.nn.gelu(spectral + accumulated + channel_bias, approximate=True).astype(jnp.bfloat16)

    return lax.map(plane_out, (x_inverse, jnp.arange(size_x, dtype=jnp.int32)))
```

```python
import functools
import math

import jax
import jax.numpy as jnp
import numpy as np
from jax import lax
from jax.experimental import pallas as pl
from jax.experimental.pallas import tpu as pltpu
from jax.sharding import PartitionSpec as P

MX = 64
MY = 16
MZ = 16
MESH = pl.DeviceIdType.MESH
ANY = pl.BlockSpec(memory_space=pl.ANY)
BF = jnp.bfloat16
F32 = jnp.float32


def signed(count):
    position = np.arange(count)
    return np.where(position < count // 2, position, position - count)


def angles(first, second, length):
    return (np.multiply.outer(first, second) % length) * (2.0 * math.pi / length)


def rounded(values):
    return np.asarray(values, dtype=BF)


def tables(count_x, count_y, cells_x, cells_y, cells_z):
    full_x, full_y = count_x * cells_x, count_y * cells_y
    half = count_y // 2
    theta = angles(np.arange(cells_z), np.arange(MZ), cells_z)
    forward = [
        rounded(f(theta) * s * cells_z**-0.5).astype(np.float64) for f, s in ((np.cos, 1), (np.sin, -1))
    ]
    backward = [
        rounded(f(theta) * s * MZ**-0.5).astype(np.float64) for f, s in ((np.cos, 1), (np.sin, -1))
    ]
    phi = angles(signed(MY), np.arange(cells_y), full_y)
    cos, sin = np.cos(phi), np.sin(phi)
    outer = lambda a, b: np.einsum("jy,zk->jkyz", a, b)
    a_re = (outer(cos, forward[0]) + outer(sin, forward[1])) * full_y**-0.5
    a_im = (outer(cos, forward[1]) - outer(sin, forward[0])) * full_y**-0.5
    b_re = (outer(cos, backward[0]) + outer(sin, backward[1])) * MY**-0.5
    b_im = (outer(cos, backward[1]) - outer(sin, backward[0])) * MY**-0.5
    band = MY // count_y
    cells = cells_y * cells_z
    split = (half, 2, band, MZ, cells)
    a = np.stack([a_re.reshape(split), a_im.reshape(split)])
    a = a.transpose(2, 1, 0, 3, 4, 5).reshape(2 * MY * MZ, cells)
    b = np.stack([b_re.reshape(split), b_im.reshape(split)])
    b = b.transpose(0, 2, 1, 3, 4, 5).reshape(2 * MY * MZ, cells).T
    theta = angles(signed(MX), np.arange(full_x), full_x)
    t = np.concatenate([np.cos(theta), np.sin(theta)]) * full_x**-0.5
    cos, sin = np.cos(theta.T), np.sin(theta.T)
    ix = np.stack([np.stack([cos, -sin]), np.stack([sin, cos])]) * MX**-0.5
    ix = ix.reshape(2, 2, count_x, cells_x, MX // 8, 8).transpose(2, 0, 3, 4, 1, 5)
    ix = ix.reshape(2 * full_x, 2 * MX)
    return tuple(rounded(v) for v in (a, b, t, ix))


def eighth(t):
    r = math.sqrt(0.5)

    def value(t):
        return jnp.where(
            t == 0,
            1.0,
            jnp.where(
                t == 4,
                -1.0,
                jnp.where((t == 2) | (t == 6), 0.0, jnp.where((t == 1) | (t == 7), r, -r)),
            ),
        ).astype(F32)

    return value(t), value((t + 6) % 8)


def kernel(
    nx, ny,
    flow, weight, conv_w, bias, a_hbm, b_hbm, t_hbm, ix_hbm,
    out,
    pad, w_v, cw_v, a_v, b_v, t_v, ix_v, brot,
    snd1, own1, rcv1, snd2, rcv2, stage, snda, rcva, sndb, rcvb, coef, conv,
    load_sem, halo_s, halo_r, pair_s, pair_r, ring_s, ring_r, a2a_s, a2a_r, ag_s, ag_r, fw_s, fw_r,
):
    gx, gy = lax.axis_index("gx"), lax.axis_index("gy")
    zh, core = gy // 2, gy % 2
    nz = ny // 2
    cx = flow.shape[0]
    cy = flow.shape[1]
    cz = flow.shape[2]
    cells = cy * cz

    loads = [
        pltpu.make_async_copy(flow, pad.at[pl.ds(1, cx), pl.ds(1, cy)], load_sem.at[0]),
        pltpu.make_async_copy(a_hbm, a_v, load_sem.at[1]),
        pltpu.make_async_copy(conv_w, cw_v, load_sem.at[2]),
        pltpu.make_async_copy(b_hbm, b_v, load_sem.at[3]),
        pltpu.make_async_copy(t_hbm, t_v, load_sem.at[4]),
        pltpu.make_async_copy(ix_hbm, ix_v, load_sem.at[5]),
        pltpu.make_async_copy(weight, w_v, load_sem.at[6]),
    ]
    for load in loads:
        load.start()

    barrier = pltpu.get_barrier_semaphore()

    def greet(i, carry):
        pl.semaphore_signal(
            barrier, inc=1, device_id=((gx + i) % nx, gy), device_id_type=MESH
        )
        return carry

    lax.fori_loop(1, nx, greet, 0)
    partner = gy + 1 - 2 * core
    beside = (gy + ny - 1 + 2 * core) % ny
    for d in range(1, nz):
        pl.semaphore_signal(
            barrier, inc=1, device_id=(gx, ((zh + d) % nz) * 2 + core), device_id_type=MESH
        )
    for y in (partner, beside):
        for dx in (0, 1, nx - 1):
            pl.semaphore_signal(
                barrier, inc=1, device_id=((gx + dx) % nx, y), device_id_type=MESH
            )

    zero_plane = jnp.zeros((cy + 2, cz, 128), BF)
    zero_row = jnp.zeros((cx + 2, 1, cz, 128), BF)

    @pl.when(gx == 0)
    def _():
        pad[0] = zero_plane

    @pl.when(gx == nx - 1)
    def _():
        pad[cx + 1] = zero_plane

    @pl.when(gy == 0)
    def _():
        pad[:, 0:1] = zero_row

    @pl.when(gy == ny - 1)
    def _():
        pad[:, cy + 1 : cy + 2] = zero_row

    loads[0].wait()
    loads[1].wait()

    def forward(half, save):
        base = pl.multiple_of(half * (ny // 2) * 64, (ny // 2) * 64)
        rows = a_v[pl.ds(base, nz * 64), :]
        spins = [[eighth(((2 * (2 * z + half) + j2) * gy) % 8) for j2 in range(2)] for z in range(nz)]
        for xp in range(cx // 2):
            rhs = jnp.concatenate(
                [pad[1 + 2 * xp + i, 1 : cy + 1].reshape(cells, 128) for i in range(2)], axis=1
            )
            y = jnp.dot(rows, rhs, preferred_element_type=F32)
            for z in range(nz):
                for j2 in range(2):
                    c, s = spins[z][j2]
                    r0 = z * 64 + j2 * 16
                    re, im = y[r0 : r0 + 16], y[r0 + 32 : r0 + 48]
                    save(r0, xp, c * re + s * im)
                    save(r0 + 32, xp, c * im - s * re)

    def save_send(r0, xp, v):
        snd1[r0 : r0 + 16, xp * 256 : xp * 256 + 256] = v.astype(BF)

    def save_own(r0, xp, v):
        own1[r0 : r0 + 16, xp * 256 : xp * 256 + 256] = v

    forward(1 - core, save_send)

    pl.semaphore_wait(barrier, nx - 1 + nz - 1 + 6)

    pair = pltpu.make_async_remote_copy(
        src_ref=snd1, dst_ref=rcv1, send_sem=pair_s, recv_sem=pair_r,
        device_id=(gx, partner), device_id_type=MESH,
    )
    pair.start()

    inner_x, inner_y = pl.ds(1, cx), pl.ds(1, cy)

    def place(step, count, inner, send):
        if step == 0:
            return inner
        edge = (count if step > 0 else 1) if send else (0 if step > 0 else count + 1)
        return pl.ds(edge, 1)

    halos = []
    for n, (dx, dy) in enumerate(
        ((0, 1), (0, -1), (1, 1), (1, -1), (-1, 1), (-1, -1), (1, 0), (-1, 0))
    ):
        ok_send = (gx + dx >= 0) & (gx + dx < nx) & (gy + dy >= 0) & (gy + dy < ny)
        ok_recv = (gx - dx >= 0) & (gx - dx < nx) & (gy - dy >= 0) & (gy - dy < ny)
        copy = pltpu.make_async_remote_copy(
            src_ref=pad.at[place(dx, cx, inner_x, True), place(dy, cy, inner_y, True)],
            dst_ref=pad.at[place(dx, cx, inner_x, False), place(dy, cy, inner_y, False)],
            send_sem=halo_s.at[n], recv_sem=halo_r.at[n],
            device_id=((gx + dx + nx) % nx, (gy + dy + ny) % ny), device_id_type=MESH,
        )
        halos.append((copy, ok_send, ok_recv))

        @pl.when(ok_send)
        def _(copy=copy):
            copy.start()

    forward(core, save_own)

    pair.wait()
    ring = []
    for d in (2, 1, 3):
        target = (zh + d) % nz
        rows = pl.ds(pl.multiple_of(target * 64, 64), 64)
        snd2[rows, :] = (own1[rows, :] + rcv1[rows, :].astype(F32)).astype(BF)
        copy = pltpu.make_async_remote_copy(
            src_ref=snd2.at[rows], dst_ref=rcv2.at[d - 1],
            send_sem=ring_s.at[d - 1], recv_sem=ring_r.at[d - 1],
            device_id=(gx, target * 2 + core), device_id_type=MESH,
        )
        copy.start()
        ring.append(copy)

    loads[2].wait()

    def conv_block(x, m):
        steps = 4
        rows_y = cy // steps
        lhs = jnp.concatenate(
            [
                pad[x + a, pl.ds(m * rows_y + b, rows_y)].reshape(rows_y * cz, 128)
                for a in range(3)
                for b in range(3)
            ],
            axis=1,
        )
        rhs = jnp.concatenate(
            [jnp.concatenate([cw_v[ab * 3 + d] for d in range(3)], axis=1) for ab in range(9)], axis=0
        )
        acc = jnp.dot(lhs, rhs, preferred_element_type=F32)
        z = lax.broadcasted_iota(jnp.int32, (rows_y * cz, 128), 0) % cz
        low = pltpu.roll(acc[:, 0:128], 1, axis=0)
        high = pltpu.roll(acc[:, 256:384], rows_y * cz - 1, axis=0)
        total = acc[:, 128:256] + jnp.where(z == 0, 0.0, low) + jnp.where(z == cz - 1, 0.0, high)
        start = pl.multiple_of(m * rows_y * cz, rows_y * cz)
        conv[x, pl.ds(start, rows_y * cz), :] = total + bias[...]

    def conv_planes(first, count):
        def step(i, carry):
            conv_block(first + i // 4, i % 4)
            return carry

        lax.fori_loop(0, count * 4, step, 0)

    def wait_halos(which):
        for n in which:
            copy, ok_send, ok_recv = halos[n]

            @pl.when(ok_recv)
            def _(copy=copy):
                copy.wait_recv()

            @pl.when(ok_send)
            def _(copy=copy):
                copy.wait_send()

    wait_halos((0, 1))
    conv_planes(1, 2)

    for copy in ring:
        copy.wait_recv()
    rows = pl.ds(pl.multiple_of(zh * 64, 64), 64)
    lane = lax.broadcasted_iota(jnp.int32, (32, 128), 1)
    for x in range(cx):
        cols = slice(x * 128, x * 128 + 128)
        band = own1[rows, cols] + rcv1[rows, cols].astype(F32)
        for d in range(nz - 1):
            band = band + rcv2[d, :, cols].astype(F32)
        re, im = band[:32], band[32:]
        stage[pl.ds(x, 32, stride=8), :] = jnp.where(lane < 64, re, pltpu.roll(im, 64, axis=1))
        stage[pl.ds(4 + x, 32, stride=8), :] = jnp.where(lane < 64, pltpu.roll(re, 64, axis=1), im)
    snda[...] = stage[...].astype(BF).reshape(nx, 4, 128)

    def exchange(src, dst, number):
        def send(i, carry):
            to = (gx + i) % nx
            pltpu.make_async_remote_copy(
                src_ref=src.at[to], dst_ref=dst.at[gx],
                send_sem=a2a_s.at[number], recv_sem=a2a_r.at[number],
                device_id=(to, gy), device_id_type=MESH,
            ).start()
            return carry

        lax.fori_loop(1, nx, send, 0)
        dst[gx] = src[gx]

    def wait_exchange(src, dst, number):
        most = pl.ds(0, nx - 1)
        done = pltpu.make_async_remote_copy(
            src_ref=src.at[most], dst_ref=dst.at[most],
            send_sem=a2a_s.at[number], recv_sem=a2a_r.at[number],
            device_id=(gx, gy), device_id_type=MESH,
        )
        done.wait_recv()
        return done

    exchange(snda, rcva, 0)

    wait_halos((2, 3, 4, 5, 6, 7))
    conv_planes(0, 1)
    conv_planes(3, 1)
    loads[3].wait()
    lanes = lax.broadcasted_iota(jnp.int32, (1, MY * MZ), 1)
    mode = 2 * (2 * ((lanes // 32) % nz) + lanes // (32 * nz)) + (lanes // 16) % 2
    spin_c, spin_s = eighth((mode * gy) % 8)

    def rotate(i, carry):
        rows = pl.ds(pl.multiple_of(i * 64, 64), 64)
        re = b_v[rows, 0:256].astype(F32)
        im = b_v[rows, 256:512].astype(F32)
        brot[rows, 0:256] = (spin_c * re + spin_s * im).astype(BF)
        brot[rows, 256:512] = (spin_c * im - spin_s * re).astype(BF)
        return carry

    lax.fori_loop(0, cells // 64, rotate, 0)
    for load in loads[4:]:
        load.wait()

    first = wait_exchange(snda, rcva, 0)
    g = rcva[...].reshape(nx * 4, 128)
    p = jnp.dot(t_v[...], g, preferred_element_type=F32)
    lane = lax.broadcasted_iota(jnp.int32, (MX, 128), 1)
    sign = jnp.where(lane < 64, 1.0, -1.0).astype(F32)
    spec = p[:MX] + sign * pltpu.roll(p[MX:], 64, axis=1)
    row0 = spec * sign
    row1 = pltpu.roll(spec, 64, axis=1)
    sub = lax.broadcasted_iota(jnp.int32, (16, 128), 0) % 8
    mixed = []
    for blk in range(MX // 8):
        rows16 = jnp.concatenate([row0[blk * 8 : blk * 8 + 8], row1[blk * 8 : blk * 8 + 8]], axis=0)
        lhs = jnp.concatenate(
            [jnp.where(sub == i, rows16, 0.0).astype(BF) for i in range(8)], axis=1
        )
        rhs = w_v[blk * 8 : blk * 8 + 8].reshape(8 * 128, 128)
        mixed.append(jnp.dot(lhs, rhs, preferred_element_type=F32))
    mixed = jnp.concatenate(mixed, axis=0).astype(BF)
    back = jnp.dot(ix_v[...], mixed, preferred_element_type=F32)
    sndb[...] = back.astype(BF).reshape(nx, 8, 128)
    exchange(sndb, rcvb, 1)
    second = wait_exchange(sndb, rcvb, 1)

    both = rcvb[...].astype(F32).reshape(nx // 2, 2, 8, 128)
    stage[...] = (both[:, 0] + both[:, 1]).reshape(nx // 2 * 8, 128)
    slot = core * nz + zh
    for q in range(2):
        for x in range(cx):
            coef[q, slot, :, x * 128 : x * 128 + 128] = stage[
                pl.ds(q * 4 + x, 32, stride=8), :
            ].astype(BF)
    gathers = []
    for d in (2, 1, 3):
        copy = pltpu.make_async_remote_copy(
            src_ref=coef.at[:, slot], dst_ref=coef.at[:, slot],
            send_sem=ag_s.at[d - 1], recv_sem=ag_r.at[d - 1],
            device_id=(gx, ((zh + d) % nz) * 2 + core), device_id_type=MESH,
        )
        copy.start()
        gathers.append(copy)
    passes = []

    def pass_on(d):
        there = core * nz + (zh - d + nz) % nz
        copy = pltpu.make_async_remote_copy(
            src_ref=coef.at[:, there], dst_ref=coef.at[:, there],
            send_sem=fw_s.at[d], recv_sem=fw_r.at[d],
            device_id=(gx, partner), device_id_type=MESH,
        )
        copy.start()
        passes.append(copy)

    pass_on(0)
    for d, copy in ((1, gathers[1]), (3, gathers[2]), (2, gathers[0])):
        copy.wait_recv()
        pass_on(d)
    for copy in passes:
        copy.wait_recv()

    root = math.sqrt(2.0 / math.pi)
    parts = 4

    def finish(i, carry):
        size = cells // parts
        rows = pl.ds(pl.multiple_of(i * size, size), size)
        lhs = brot[rows, :]
        for xp in range(cx // 2):
            rhs = coef[:, :, :, xp * 256 : xp * 256 + 256].reshape(2 * MY * MZ, 256)
            acc = jnp.dot(lhs, rhs, preferred_element_type=F32)
            for x in range(2):
                v = acc[:, x * 128 : x * 128 + 128] + conv[2 * xp + x, rows, :]
                v = 0.5 * v * (1.0 + jnp.tanh(root * (v + 0.044715 * (v * v * v))))
                out[2 * xp + x, rows, :] = v.astype(BF)
        return carry

    lax.fori_loop(0, parts, finish, 0)

    for copy in ring + gathers + passes:
        copy.wait_send()
    first.wait_send()
    second.wait_send()


def body(consts, nx, ny, flow_field, spectral_weight, conv_weight, channel_bias):
    cells_x, cells_y, cells_z, channels = flow_field.shape
    cells = cells_y * cells_z
    nz = ny // 2
    modes = 2 * MY * MZ
    v = pltpu.VMEM
    dma = pltpu.SemaphoreType.DMA
    vmem = pl.BlockSpec(memory_space=pltpu.VMEM)
    out = pl.pallas_call(
        functools.partial(kernel, nx, ny),
        out_shape=jax.ShapeDtypeStruct((cells_x, cells, channels), BF),
        in_specs=[ANY, ANY, ANY, vmem, ANY, ANY, ANY, ANY],
        out_specs=vmem,
        scratch_shapes=[
            v((cells_x + 2, cells_y + 2, cells_z, channels), BF),
            v((MX, 128, 128), BF),
            v((27, 128, 128), BF),
            v((modes, cells), BF),
            v((cells, modes), BF),
            v((2 * MX, nx * cells_x), BF),
            v((2 * nx * cells_x, 2 * MX), BF),
            v((cells, modes), BF),
            v((modes // 2, cells_x * 128), BF),
            v((modes // 2, cells_x * 128), F32),
            v((modes // 2, cells_x * 128), BF),
            v((modes // 2, cells_x * 128), BF),
            v((nz - 1, 64, cells_x * 128), BF),
            v((256, 128), F32),
            v((nx, 4, 128), BF),
            v((nx, 4, 128), BF),
            v((nx, 8, 128), BF),
            v((nx, 8, 128), BF),
            v((2, ny, 32, cells_x * 128), BF),
            v((cells_x, cells, 128), F32),
            dma((7,)),
            dma((8,)),
            dma((8,)),
            dma,
            dma,
            dma((nz - 1,)),
            dma((nz - 1,)),
            dma((2,)),
            dma((2,)),
            dma((nz - 1,)),
            dma((nz - 1,)),
            dma((nz,)),
            dma((nz,)),
        ],
        compiler_params=pltpu.CompilerParams(collective_id=0, has_side_effects=True),
        name="layer",
    )(
        flow_field,
        spectral_weight.reshape(MX, 128, 128),
        conv_weight.reshape(27, 128, 128),
        channel_bias.reshape(1, channels),
        *consts,
    )
    return out.reshape(cells_x, cells_y, cells_z, channels)


def solution(mesh):
    nx, ny = mesh.shape["gx"], mesh.shape["gy"]
    consts = tables(nx, ny, 4, 16, 64)

    def layer(*args):
        return body(tuple(jnp.asarray(c) for c in consts), nx, ny, *args)

    placed = (P("gx", "gy", None, None), P(("gy", "gx"), None, None, None, None), P(), P())
    return jax.shard_map(
        layer, mesh=mesh, in_specs=placed, out_specs=P("gx", "gy", None, None), check_vma=False
    )
```

```python
import functools
import math

import jax
import jax.numpy as jnp
import numpy as np
from jax import lax
from jax.experimental import pallas as pl
from jax.experimental.pallas import tpu as pltpu
from jax.sharding import PartitionSpec as P

MX = 64
MY = 16
MZ = 16
MESH = pl.DeviceIdType.MESH
ANY = pl.BlockSpec(memory_space=pl.ANY)
BF = jnp.bfloat16
F32 = jnp.float32


def signed(count):
    position = np.arange(count)
    return np.where(position < count // 2, position, position - count)


def angles(first, second, length):
    return (np.multiply.outer(first, second) % length) * (2.0 * math.pi / length)


def rounded(values):
    return np.asarray(values, dtype=BF)


def tables(count_x, count_y, cells_x, cells_y, cells_z):
    full_x, full_y = count_x * cells_x, count_y * cells_y
    half = count_y // 2
    theta = angles(np.arange(cells_z), np.arange(MZ), cells_z)
    forward = [
        rounded(f(theta) * s * cells_z**-0.5).astype(np.float64) for f, s in ((np.cos, 1), (np.sin, -1))
    ]
    backward = [
        rounded(f(theta) * s * MZ**-0.5).astype(np.float64) for f, s in ((np.cos, 1), (np.sin, -1))
    ]
    phi = angles(signed(MY), np.arange(cells_y), full_y)
    cos, sin = np.cos(phi), np.sin(phi)
    outer = lambda a, b: np.einsum("jy,zk->jkyz", a, b)
    a_re = (outer(cos, forward[0]) + outer(sin, forward[1])) * full_y**-0.5
    a_im = (outer(cos, forward[1]) - outer(sin, forward[0])) * full_y**-0.5
    b_re = (outer(cos, backward[0]) + outer(sin, backward[1])) * MY**-0.5
    b_im = (outer(cos, backward[1]) - outer(sin, backward[0])) * MY**-0.5
    band = MY // count_y
    cells = cells_y * cells_z
    split = (half, 2, band, MZ, cells)
    a = np.stack([a_re.reshape(split), a_im.reshape(split)])
    a = a.transpose(2, 1, 0, 3, 4, 5).reshape(2 * MY * MZ, cells)
    b = np.stack([b_re.reshape(split), b_im.reshape(split)])
    b = b.transpose(0, 2, 1, 3, 4, 5).reshape(2 * MY * MZ, cells).T
    theta = angles(signed(MX), np.arange(full_x), full_x)
    t = np.concatenate([np.cos(theta), np.sin(theta)]) * full_x**-0.5
    cos, sin = np.cos(theta.T), np.sin(theta.T)
    ix = np.stack([np.stack([cos, -sin]), np.stack([sin, cos])]) * MX**-0.5
    ix = ix.reshape(2, 2, count_x, cells_x, MX // 8, 8).transpose(2, 0, 3, 4, 1, 5)
    ix = ix.reshape(2 * full_x, 2 * MX)
    return tuple(rounded(v) for v in (a, b, t, ix))


def eighth(t):
    r = math.sqrt(0.5)

    def value(t):
        return jnp.where(
            t == 0,
            1.0,
            jnp.where(
                t == 4,
                -1.0,
                jnp.where((t == 2) | (t == 6), 0.0, jnp.where((t == 1) | (t == 7), r, -r)),
            ),
        ).astype(F32)

    return value(t), value((t + 6) % 8)


def kernel(
    nx, ny,
    flow, weight, conv_w, bias_hbm, a_hbm, b_hbm, t_hbm, ix_hbm,
    out,
    pad, w_v, cw_v, bias, a_v, b_v, t_v, ix_v, brot,
    snd1, own1, rcv1, snd2, rcv2, stage, snda, rcva, sndb, rcvb, coef, conv,
    load_sem, wave, halo_s, halo_r, pair_s, pair_r, ring_s, ring_r, a2a_s, a2a_r, ag_s, ag_r, fw_s, fw_r,
):
    gx, gy = lax.axis_index("gx"), lax.axis_index("gy")
    zh, core = gy // 2, gy % 2
    nz = ny // 2
    cx = flow.shape[0]
    cy = flow.shape[1]
    cz = flow.shape[2]
    cells = cy * cz
    lx, lz, ly = nx // 16, 2, 8
    at_x, at_z, at_y = gx // 16, (gx // 8) % 2, gx % 8
    to_x = [((at_x + i) % lx) * 16 for i in range(lx)]
    to_z = [((at_z + i) % lz) * 8 for i in range(lz)]
    to_y = [(at_y + i) % ly for i in range(ly)]

    loads = [
        pltpu.make_async_copy(flow, pad.at[pl.ds(1, cx), pl.ds(1, cy)], load_sem.at[0]),
        pltpu.make_async_copy(a_hbm, a_v, load_sem.at[1]),
        pltpu.make_async_copy(b_hbm, b_v, load_sem.at[2]),
        pltpu.make_async_copy(conv_w, cw_v, load_sem.at[3]),
        pltpu.make_async_copy(bias_hbm, bias, load_sem.at[4]),
        pltpu.make_async_copy(t_hbm, t_v, load_sem.at[5]),
        pltpu.make_async_copy(weight, w_v, load_sem.at[6]),
        pltpu.make_async_copy(ix_hbm, ix_v, load_sem.at[7]),
    ]
    loads[0].start()
    loads[1].start()

    barrier = pltpu.get_barrier_semaphore()
    partner = gy + 1 - 2 * core
    beside = (gy + ny - 1 + 2 * core) % ny
    next_x, last_x = (gx + 1) % nx, (gx + nx - 1) % nx

    def peer(x, y):
        return {"device_id": (x, y), "device_id_type": MESH}

    greeted = [(gx, ((zh + d) % nz) * 2 + core) for d in range(1, nz)]
    greeted += [(to_x[0] + to_z[0] + to_y[i], gy) for i in range(1, ly)]
    greeted += [(to_x[i] + to_z[0] + to_y[0], gy) for i in range(1, lx)]
    greeted += [(to_x[0] + to_z[1] + to_y[0], gy)]
    greeted += [(x, y) for y in (partner, beside) for x in (gx, next_x, last_x)]
    greeted += [(next_x, gy), (last_x, gy)]
    for x, y in greeted:
        pl.semaphore_signal(barrier, inc=1, **peer(x, y))

    zero_plane = jnp.zeros((cy + 2, cz, 128), BF)
    zero_row = jnp.zeros((cx + 2, 1, cz, 128), BF)

    @pl.when(gx == 0)
    def _():
        pad[0] = zero_plane

    @pl.when(gx == nx - 1)
    def _():
        pad[cx + 1] = zero_plane

    @pl.when(gy == 0)
    def _():
        pad[:, 0:1] = zero_row

    @pl.when(gy == ny - 1)
    def _():
        pad[:, cy + 1 : cy + 2] = zero_row

    loads[0].wait()
    loads[1].wait()

    def forward(half, save):
        base = pl.multiple_of(half * nz * 64, nz * 64)
        rows = a_v[pl.ds(base, nz * 64), :]
        spins = [[eighth(((2 * (2 * z + half) + j2) * gy) % 8) for j2 in range(2)] for z in range(nz)]
        for xp in range(cx // 2):
            rhs = jnp.concatenate(
                [pad[1 + 2 * xp + i, 1 : cy + 1].reshape(cells, 128) for i in range(2)], axis=1
            )
            y = jnp.dot(rows, rhs, preferred_element_type=F32)
            for z in range(nz):
                for j2 in range(2):
                    c, s = spins[z][j2]
                    r0 = z * 64 + j2 * 16
                    re, im = y[r0 : r0 + 16], y[r0 + 32 : r0 + 48]
                    save(r0, xp, c * re + s * im)
                    save(r0 + 32, xp, c * im - s * re)

    def save_send(r0, xp, v):
        snd1[r0 : r0 + 16, xp * 256 : xp * 256 + 256] = v.astype(BF)

    def save_own(r0, xp, v):
        own1[r0 : r0 + 16, xp * 256 : xp * 256 + 256] = v

    forward(1 - core, save_send)
    for load in loads[2:]:
        load.start()

    pl.semaphore_wait(barrier, len(greeted))

    pairs = {}
    for d in (2, 1, 3, 0):
        rows = pl.ds(pl.multiple_of(((zh + d) % nz) * 64, 64), 64)
        pairs[d] = pltpu.make_async_remote_copy(
            src_ref=snd1.at[rows], dst_ref=rcv1.at[rows],
            send_sem=pair_s.at[d], recv_sem=pair_r.at[d], **peer(gx, partner),
        )
        pairs[d].start()
    for i in range(1, ly):
        pl.semaphore_signal(wave.at[0], inc=1, **peer(to_x[0] + to_z[0] + to_y[i], gy))

    inner_x, inner_y = pl.ds(1, cx), pl.ds(1, cy)

    def place(step, count, inner, send):
        if step == 0:
            return inner
        edge = (count if step > 0 else 1) if send else (0 if step > 0 else count + 1)
        return pl.ds(edge, 1)

    halos = []
    for n, (dx, dy) in enumerate(
        ((0, 1), (0, -1), (1, 1), (1, -1), (-1, 1), (-1, -1), (1, 0), (-1, 0))
    ):
        ok_send = (gx + dx >= 0) & (gx + dx < nx) & (gy + dy >= 0) & (gy + dy < ny)
        ok_recv = (gx - dx >= 0) & (gx - dx < nx) & (gy - dy >= 0) & (gy - dy < ny)
        copy = pltpu.make_async_remote_copy(
            src_ref=pad.at[place(dx, cx, inner_x, True), place(dy, cy, inner_y, True)],
            dst_ref=pad.at[place(dx, cx, inner_x, False), place(dy, cy, inner_y, False)],
            send_sem=halo_s.at[n], recv_sem=halo_r.at[n],
            **peer((gx + dx + nx) % nx, (gy + dy + ny) % ny),
        )
        halos.append((copy, ok_send, ok_recv))

    def start_halo(n, condition):
        @pl.when(condition)
        def _():
            halos[n][0].start()

    near = {6: at_y < ly - 1, 7: at_y > 0}
    for n in (6, 7):
        start_halo(n, halos[n][1] & near[n])

    forward(core, save_own)

    ring = []
    for d in (2, 1, 3):
        target = (zh + d) % nz
        rows = pl.ds(pl.multiple_of(target * 64, 64), 64)
        pairs[d].wait_recv()
        snd2[rows, :] = (own1[rows, :] + rcv1[rows, :].astype(F32)).astype(BF)
        copy = pltpu.make_async_remote_copy(
            src_ref=snd2.at[rows], dst_ref=rcv2.at[d - 1],
            send_sem=ring_s.at[d - 1], recv_sem=ring_r.at[d - 1],
            **peer(gx, target * 2 + core),
        )
        copy.start()
        ring.append(copy)

    loads[2].wait()
    lanes = lax.broadcasted_iota(jnp.int32, (1, MY * MZ), 1)
    mode = 2 * (2 * ((lanes // 32) % nz) + lanes // (32 * nz)) + (lanes // 16) % 2
    spin_c, spin_s = eighth((mode * gy) % 8)

    def rotate(i, carry):
        rows = pl.ds(pl.multiple_of(i * 64, 64), 64)
        re = b_v[rows, 0:256].astype(F32)
        im = b_v[rows, 256:512].astype(F32)
        brot[rows, 0:256] = (spin_c * re + spin_s * im).astype(BF)
        brot[rows, 256:512] = (spin_c * im - spin_s * re).astype(BF)
        return carry

    lax.fori_loop(0, cells // 64, rotate, 0)
    for load in loads[3:5]:
        load.wait()

    steps = 4
    rows_y = cy // steps

    def conv_block(x, m):
        lhs = jnp.concatenate(
            [
                pad[x + a, pl.ds(m * rows_y + b, rows_y)].reshape(rows_y * cz, 128)
                for a in range(3)
                for b in range(3)
            ],
            axis=1,
        )
        rhs = jnp.concatenate(
            [jnp.concatenate([cw_v[ab * 3 + d] for d in range(3)], axis=1) for ab in range(9)], axis=0
        )
        acc = jnp.dot(lhs, rhs, preferred_element_type=F32)
        z = lax.broadcasted_iota(jnp.int32, (rows_y * cz, 128), 0) % cz
        low = pltpu.roll(acc[:, 0:128], 1, axis=0)
        high = pltpu.roll(acc[:, 256:384], rows_y * cz - 1, axis=0)
        total = acc[:, 128:256] + jnp.where(z == 0, 0.0, low) + jnp.where(z == cz - 1, 0.0, high)
        start = pl.multiple_of(m * rows_y * cz, rows_y * cz)
        conv[x, pl.ds(start, rows_y * cz), :] = total + bias[...]

    def conv_blocks(count, place):
        def step(i, carry):
            conv_block(*place(i))
            return carry

        lax.fori_loop(0, count, step, 0)

    conv_blocks(2, lambda i: (1 + i, 1))

    pl.semaphore_wait(wave.at[0], ly - 1)
    pl.semaphore_signal(wave.at[1], inc=1, **peer(to_x[0] + to_z[1] + to_y[0], gy))

    pairs[0].wait_recv()
    for copy in ring:
        copy.wait_recv()

    rows = pl.ds(pl.multiple_of(zh * 64, 64), 64)
    lane = lax.broadcasted_iota(jnp.int32, (32, 128), 1)
    for x in range(cx):
        cols = slice(x * 128, x * 128 + 128)
        band = own1[rows, cols] + rcv1[rows, cols].astype(F32)
        for d in range(nz - 1):
            band = band + rcv2[d, :, cols].astype(F32)
        re, im = band[:32], band[32:]
        stage[pl.ds(x, 32, stride=8), :] = jnp.where(lane < 64, re, pltpu.roll(im, 64, axis=1))
        stage[pl.ds(4 + x, 32, stride=8), :] = jnp.where(lane < 64, pltpu.roll(re, 64, axis=1), im)
    snda[...] = stage[...].astype(BF).reshape(nx, 4, 128)

    pl.semaphore_wait(wave.at[1], 1)

    hops = lambda i, n: min(i, n - i)
    order = [(x, z, y) for x in range(lx) for z in range(lz) for y in range(ly)]
    order.sort(key=lambda o: -(hops(o[0], lx) + hops(o[1], lz) + hops(o[2], ly)))

    def exchange(src, dst, number):
        for x, z, y in order[:-1]:
            to = to_x[x] + to_z[z] + to_y[y]
            pltpu.make_async_remote_copy(
                src_ref=src.at[to], dst_ref=dst.at[gx],
                send_sem=a2a_s.at[number], recv_sem=a2a_r.at[number], **peer(to, gy),
            ).start()
        dst[gx] = src[gx]

    def wait_exchange(src, dst, number):
        most = pl.ds(0, nx - 1)
        done = pltpu.make_async_remote_copy(
            src_ref=src.at[most], dst_ref=dst.at[most],
            send_sem=a2a_s.at[number], recv_sem=a2a_r.at[number], **peer(gx, gy),
        )
        done.wait_recv()
        return done

    exchange(snda, rcva, 0)

    for n in range(6):
        start_halo(n, halos[n][1])
    for n in (6, 7):
        start_halo(n, halos[n][1] & jnp.logical_not(near[n]))

    conv_blocks(2, lambda i: (1 + i, 2))
    for load in loads[5:]:
        load.wait()

    first = wait_exchange(snda, rcva, 0)

    g = rcva[...].reshape(nx * 4, 128)
    p = jnp.dot(t_v[...], g, preferred_element_type=F32)
    lane = lax.broadcasted_iota(jnp.int32, (MX, 128), 1)
    sign = jnp.where(lane < 64, 1.0, -1.0).astype(F32)
    spec = p[:MX] + sign * pltpu.roll(p[MX:], 64, axis=1)

    row0 = spec * sign
    row1 = pltpu.roll(spec, 64, axis=1)
    sub = lax.broadcasted_iota(jnp.int32, (16, 128), 0) % 8
    mixed = []
    for blk in range(MX // 8):
        rows16 = jnp.concatenate([row0[blk * 8 : blk * 8 + 8], row1[blk * 8 : blk * 8 + 8]], axis=0)
        lhs = jnp.concatenate(
            [jnp.where(sub == i, rows16, 0.0).astype(BF) for i in range(8)], axis=1
        )
        rhs = w_v[blk * 8 : blk * 8 + 8].reshape(8 * 128, 128)
        mixed.append(jnp.dot(lhs, rhs, preferred_element_type=F32))
    mixed = jnp.concatenate(mixed, axis=0).astype(BF)

    back = jnp.dot(ix_v[...], mixed, preferred_element_type=F32)
    sndb[...] = back.astype(BF).reshape(nx, 8, 128)

    exchange(sndb, rcvb, 1)

    for copy, ok_send, ok_recv in halos:
        @pl.when(ok_recv)
        def _(copy=copy):
            copy.wait_recv()

    conv_blocks(4, lambda i: (1 + i % 2, 3 * (i // 2)))
    conv_blocks(4, lambda i: (0, i))

    second = wait_exchange(sndb, rcvb, 1)

    both = rcvb[...].astype(F32).reshape(nx // 2, 2, 8, 128)
    stage[...] = (both[:, 0] + both[:, 1]).reshape(nx // 2 * 8, 128)
    slot = core * nz + zh
    for q in range(2):
        for x in range(cx):
            coef[q, slot, :, x * 128 : x * 128 + 128] = stage[
                pl.ds(q * 4 + x, 32, stride=8), :
            ].astype(BF)

    gathers = []
    for d in (2, 1, 3):
        copy = pltpu.make_async_remote_copy(
            src_ref=coef.at[:, slot], dst_ref=coef.at[:, slot],
            send_sem=ag_s.at[d - 1], recv_sem=ag_r.at[d - 1],
            **peer(gx, ((zh + d) % nz) * 2 + core),
        )
        copy.start()
        gathers.append(copy)
    passes = []

    def pass_on(d):
        there = core * nz + (zh - d + nz) % nz
        copy = pltpu.make_async_remote_copy(
            src_ref=coef.at[:, there], dst_ref=coef.at[:, there],
            send_sem=fw_s.at[d], recv_sem=fw_r.at[d], **peer(gx, partner),
        )
        copy.start()
        passes.append(copy)

    pass_on(0)

    conv_blocks(4, lambda i: (cx - 1, i))

    for d, copy in ((1, gathers[1]), (3, gathers[2]), (2, gathers[0])):
        copy.wait_recv()
        pass_on(d)

    for copy in passes:
        copy.wait_recv()

    root = math.sqrt(2.0 / math.pi)
    parts = 4

    def finish(i, carry):
        size = cells // parts
        rows = pl.ds(pl.multiple_of(i * size, size), size)
        lhs = brot[rows, :]
        for xp in range(cx // 2):
            rhs = coef[:, :, :, xp * 256 : xp * 256 + 256].reshape(2 * MY * MZ, 256)
            acc = jnp.dot(lhs, rhs, preferred_element_type=F32)
            for x in range(2):
                v = acc[:, x * 128 : x * 128 + 128] + conv[2 * xp + x, rows, :]
                v = 0.5 * v * (1.0 + jnp.tanh(root * (v + 0.044715 * (v * v * v))))
                out[2 * xp + x, rows, :] = v.astype(BF)
        return carry

    lax.fori_loop(0, parts, finish, 0)

    for copy in list(pairs.values()) + ring + gathers + passes:
        copy.wait_send()
    first.wait_send()
    second.wait_send()
    for copy, ok_send, ok_recv in halos:
        @pl.when(ok_send)
        def _(copy=copy):
            copy.wait_send()


def body(consts, nx, ny, flow_field, spectral_weight, conv_weight, channel_bias):
    cells_x, cells_y, cells_z, channels = flow_field.shape
    cells = cells_y * cells_z
    nz = ny // 2
    modes = 2 * MY * MZ
    v = pltpu.VMEM
    dma = pltpu.SemaphoreType.DMA
    vmem = pl.BlockSpec(memory_space=pltpu.VMEM)
    out = pl.pallas_call(
        functools.partial(kernel, nx, ny),
        out_shape=pltpu.VMEM((cells_x, cells, channels), BF),
        in_specs=[ANY] * 8,
        out_specs=vmem,
        scratch_shapes=[
            v((cells_x + 2, cells_y + 2, cells_z, channels), BF),
            v((MX, 128, 128), BF),
            v((27, 128, 128), BF),
            v((1, channels), F32),
            v((modes, cells), BF),
            v((cells, modes), BF),
            v((2 * MX, nx * cells_x), BF),
            v((2 * nx * cells_x, 2 * MX), BF),
            v((cells, modes), BF),
            v((modes // 2, cells_x * 128), BF),
            v((modes // 2, cells_x * 128), F32),
            v((modes // 2, cells_x * 128), BF),
            v((modes // 2, cells_x * 128), BF),
            v((nz - 1, 64, cells_x * 128), BF),
            v((256, 128), F32),
            v((nx, 4, 128), BF),
            v((nx, 4, 128), BF),
            v((nx, 8, 128), BF),
            v((nx, 8, 128), BF),
            v((2, ny, 32, cells_x * 128), BF),
            v((cells_x, cells, 128), F32),
            dma((8,)),
            pltpu.SemaphoreType.REGULAR((2,)),
            dma((8,)),
            dma((8,)),
            dma((nz,)),
            dma((nz,)),
            dma((nz - 1,)),
            dma((nz - 1,)),
            dma((2,)),
            dma((2,)),
            dma((nz - 1,)),
            dma((nz - 1,)),
            dma((nz,)),
            dma((nz,)),
        ],
        compiler_params=pltpu.CompilerParams(collective_id=0, has_side_effects=True),
        name="layer",
    )(
        flow_field,
        spectral_weight.reshape(MX, 128, 128),
        conv_weight.reshape(27, 128, 128),
        channel_bias.reshape(1, channels),
        *consts,
    )
    return out.reshape(cells_x, cells_y, cells_z, channels)


def solution(mesh):
    nx, ny = mesh.shape["gx"], mesh.shape["gy"]
    consts = tables(nx, ny, 4, 16, 64)

    def layer(*args):
        return body(tuple(jnp.asarray(c) for c in consts), nx, ny, *args)

    placed = (P("gx", "gy", None, None), P(("gy", "gx"), None, None, None, None), P(), P())
    return jax.shard_map(
        layer, mesh=mesh, in_specs=placed, out_specs=P("gx", "gy", None, None), check_vma=False
    )
```

```python
import functools
import math

import jax
import jax.numpy as jnp
import numpy as np
from jax import lax
from jax.experimental import pallas as pl
from jax.experimental.pallas import tpu as pltpu
from jax.sharding import PartitionSpec as P

MX = 64
MY = 16
MZ = 16
MESH = pl.DeviceIdType.MESH
ANY = pl.BlockSpec(memory_space=pl.ANY)
BF = jnp.bfloat16
F32 = jnp.float32


def signed(count):
    position = np.arange(count)
    return np.where(position < count // 2, position, position - count)


def angles(first, second, length):
    return (np.multiply.outer(first, second) % length) * (2.0 * math.pi / length)


def rounded(values):
    return np.asarray(values, dtype=BF)


def tables(count_x, count_y, cells_x, cells_y, cells_z):
    full_x, full_y = count_x * cells_x, count_y * cells_y
    half = count_y // 2
    theta = angles(np.arange(cells_z), np.arange(MZ), cells_z)
    forward = [
        rounded(f(theta) * s * cells_z**-0.5).astype(np.float64) for f, s in ((np.cos, 1), (np.sin, -1))
    ]
    backward = [
        rounded(f(theta) * s * MZ**-0.5).astype(np.float64) for f, s in ((np.cos, 1), (np.sin, -1))
    ]
    phi = angles(signed(MY), np.arange(cells_y), full_y)
    cos, sin = np.cos(phi), np.sin(phi)
    outer = lambda a, b: np.einsum("jy,zk->jkyz", a, b)
    a_re = (outer(cos, forward[0]) + outer(sin, forward[1])) * full_y**-0.5
    a_im = (outer(cos, forward[1]) - outer(sin, forward[0])) * full_y**-0.5
    b_re = (outer(cos, backward[0]) + outer(sin, backward[1])) * MY**-0.5
    b_im = (outer(cos, backward[1]) - outer(sin, backward[0])) * MY**-0.5
    band = MY // count_y
    cells = cells_y * cells_z
    split = (half, 2, band, MZ, cells)
    a = np.stack([a_re.reshape(split), a_im.reshape(split)])
    a = a.transpose(2, 1, 0, 3, 4, 5).reshape(2 * MY * MZ, cells)
    b = np.stack([b_re.reshape(split), b_im.reshape(split)])
    b = b.transpose(0, 2, 1, 3, 4, 5).reshape(2 * MY * MZ, cells).T
    theta = angles(signed(MX), np.arange(full_x), full_x)
    t = np.concatenate([np.cos(theta), np.sin(theta)]) * full_x**-0.5
    cos, sin = np.cos(theta.T), np.sin(theta.T)
    ix = np.stack([np.stack([cos, -sin]), np.stack([sin, cos])]) * MX**-0.5
    ix = ix.reshape(2, 2, count_x, cells_x, MX // 8, 8).transpose(2, 0, 3, 4, 1, 5)
    ix = ix.reshape(2 * full_x, 2 * MX)
    x = np.concatenate([ix, t[:, :128], t[:, 128:]])
    return tuple(rounded(v) for v in (a, b, x))


def eighth(t):
    r = math.sqrt(0.5)

    def value(t):
        return jnp.where(
            t == 0,
            1.0,
            jnp.where(
                t == 4,
                -1.0,
                jnp.where((t == 2) | (t == 6), 0.0, jnp.where((t == 1) | (t == 7), r, -r)),
            ),
        ).astype(F32)

    return value(t), value((t + 6) % 8)


def kernel(
    nx, ny,
    flow, weight, conv_w, bias_hbm, a_hbm, b_hbm, x_hbm,
    out,
    pad, w_v, cw_v, bias, a_v, b_v, x_v, brot,
    snd1, own1, rcv1, snd2, rcv2, stage, snda, rcva, sndb, rcvb, coef, conv, sizes,
    load_sem, wave, sent, halo_s, halo_r, pair_r, ring_r, a2a_r, ag_r, fw_r,
):
    gx, gy = lax.axis_index("gx"), lax.axis_index("gy")
    zh, core = gy // 2, gy % 2
    nz = ny // 2
    cx = flow.shape[0]
    cy = flow.shape[1]
    cz = flow.shape[2]
    cells = cy * cz
    lx, lz, ly = nx // 16, 2, 8
    at_x, at_z, at_y = gx // 16, (gx // 8) % 2, gx % 8
    to_x = [((at_x + i) % lx) * 16 for i in range(lx)]
    to_z = [((at_z + i) % lz) * 8 for i in range(lz)]
    to_y = [(at_y + i) % ly for i in range(ly)]

    half_rows = nz * 64
    first_rows = pl.ds(pl.multiple_of((1 - core) * half_rows, half_rows), half_rows)
    other_rows = pl.ds(pl.multiple_of(core * half_rows, half_rows), half_rows)

    def load(source, target, number):
        return pltpu.make_async_copy(source, target, load_sem.at[number])

    load_flow = load(flow, pad.at[pl.ds(1, cx), pl.ds(1, cy)], 0)
    load_first = load(a_hbm.at[first_rows], a_v.at[first_rows], 1)
    load_other = load(a_hbm.at[other_rows], a_v.at[other_rows], 2)
    load_back = load(b_hbm, b_v, 0)
    load_conv = load(conv_w, cw_v, 1)
    load_bias = load(bias_hbm, bias, 3)
    load_weight = load(weight, w_v, 4)
    load_x = load(x_hbm, x_v, 5)
    load_first.start()
    load_flow.start()
    load_other.start()

    barrier = pltpu.get_barrier_semaphore()
    partner = gy + 1 - 2 * core
    beside = (gy + ny - 1 + 2 * core) % ny
    next_x, last_x = (gx + 1) % nx, (gx + nx - 1) % nx

    def peer(x, y):
        return {"device_id": (x, y), "device_id_type": MESH}

    greeted = [(gx, ((zh + d) % nz) * 2 + core) for d in range(1, nz)]
    greeted += [(to_x[0] + to_z[0] + to_y[i], gy) for i in range(1, ly)]
    greeted += [(to_x[i] + to_z[0] + to_y[0], gy) for i in range(1, lx)]
    greeted += [(to_x[0] + to_z[1] + to_y[0], gy)]
    greeted += [(x, y) for y in (partner, beside) for x in (gx, next_x, last_x)]
    greeted += [(next_x, gy), (last_x, gy)]
    for x, y in greeted:
        pl.semaphore_signal(barrier, inc=1, **peer(x, y))

    zero_plane = jnp.zeros((cy + 2, cz, 128), BF)
    zero_row = jnp.zeros((cx + 2, 1, cz, 128), BF)

    @pl.when(gx == 0)
    def _():
        pad[0] = zero_plane

    @pl.when(gx == nx - 1)
    def _():
        pad[cx + 1] = zero_plane

    @pl.when(gy == 0)
    def _():
        pad[:, 0:1] = zero_row

    @pl.when(gy == ny - 1)
    def _():
        pad[:, cy + 1 : cy + 2] = zero_row

    load_first.wait()
    load_flow.wait()

    order_z = (2, 1, 3, 0)

    def send(source, target, recv_sem, device):
        copy = pltpu.make_async_remote_copy(
            src_ref=source, dst_ref=target, send_sem=sent, recv_sem=recv_sem, **device
        )
        copy.start()
        return copy

    def forward(half, save):
        targets = [(zh + d) % nz for d in order_z]
        rows = jnp.concatenate(
            [a_v[pl.ds(pl.multiple_of((half * nz + z) * 64, 64), 64), :] for z in targets], axis=0
        )
        spins = [[eighth(((2 * (2 * z + half) + j2) * gy) % 8) for j2 in range(2)] for z in targets]
        for xp in range(cx // 2):
            rhs = jnp.concatenate(
                [pad[1 + 2 * xp + i, 1 : cy + 1].reshape(cells, 128) for i in range(2)], axis=1
            )
            y = jnp.dot(rows, rhs, preferred_element_type=F32)
            for n in range(nz):
                for j2 in range(2):
                    c, s = spins[n][j2]
                    r0 = n * 64 + j2 * 16
                    re, im = y[r0 : r0 + 16], y[r0 + 32 : r0 + 48]
                    save(r0, xp, c * re + s * im)
                    save(r0 + 32, xp, c * im - s * re)

    def save_send(r0, xp, v):
        snd1[r0 : r0 + 16, xp * 256 : xp * 256 + 256] = v.astype(BF)

    def save_own(r0, xp, v):
        own1[r0 : r0 + 16, xp * 256 : xp * 256 + 256] = v

    forward(1 - core, save_send)
    for item in (load_back, load_conv, load_bias, load_weight, load_x):
        item.start()

    pl.semaphore_wait(barrier, len(greeted))

    pair_rows = (pl.ds(0, 64), pl.ds(64, (nz - 1) * 64))
    pairs = [
        send(snd1.at[rows], rcv1.at[rows], pair_r.at[n], peer(gx, partner))
        for n, rows in enumerate(pair_rows)
    ]
    for i in range(1, ly):
        pl.semaphore_signal(wave.at[0], inc=1, **peer(to_x[0] + to_z[0] + to_y[i], gy))

    inner_x, inner_y = pl.ds(1, cx), pl.ds(1, cy)

    def place(step, count, inner, send):
        if step == 0:
            return inner
        edge = (count if step > 0 else 1) if send else (0 if step > 0 else count + 1)
        return pl.ds(edge, 1)

    steps = ((0, 1), (0, -1), (1, 1), (1, -1), (-1, 1), (-1, -1), (1, 0), (-1, 0))

    def halo(n):
        dx, dy = steps[n]
        return pltpu.make_async_remote_copy(
            src_ref=pad.at[place(dx, cx, inner_x, True), place(dy, cy, inner_y, True)],
            dst_ref=pad.at[place(dx, cx, inner_x, False), place(dy, cy, inner_y, False)],
            send_sem=halo_s.at[n], recv_sem=halo_r.at[n],
            **peer((gx + dx + nx) % nx, (gy + dy + ny) % ny),
        )

    def inside_grid(n, sign):
        dx, dy = steps[n]
        x, y = gx + sign * dx, gy + sign * dy
        return (x >= 0) & (x < nx) & (y >= 0) & (y < ny)

    def start_halo(n, condition=True):
        @pl.when(inside_grid(n, 1) & condition)
        def _():
            halo(n).start()

    def wait_halo(n, condition=True):
        @pl.when(inside_grid(n, -1) & condition)
        def _():
            halo(n).wait_recv()

    near = {6: at_y < ly - 1, 7: at_y > 0}
    for n in (6, 7):
        start_halo(n, near[n])

    load_other.wait()
    forward(core, save_own)

    for n, d in enumerate(order_z[:-1]):
        rows = slice(n * 64, n * 64 + 64)
        if n < 2:
            pairs[n].wait_recv()
        snd2[rows, :] = (own1[rows, :] + rcv1[rows, :].astype(F32)).astype(BF)
        send(snd2.at[rows], rcv2.at[n], ring_r, peer(gx, ((zh + d) % nz) * 2 + core))

    load_back.wait()
    lanes = lax.broadcasted_iota(jnp.int32, (1, MY * MZ), 1)
    mode = 2 * (2 * ((lanes // 32) % nz) + lanes // (32 * nz)) + (lanes // 16) % 2
    spin_c, spin_s = eighth((mode * gy) % 8)

    def rotate(i, carry):
        rows = pl.ds(pl.multiple_of(i * 64, 64), 64)
        re = b_v[rows, 0:256].astype(F32)
        im = b_v[rows, 256:512].astype(F32)
        brot[rows, 0:256] = (spin_c * re + spin_s * im).astype(BF)
        brot[rows, 256:512] = (spin_c * im - spin_s * re).astype(BF)
        return carry

    lax.fori_loop(0, cells // 64, rotate, 0)
    load_conv.wait()
    load_bias.wait()

    rows_y = cy // 4

    def conv_block(x, m):
        lhs = jnp.concatenate(
            [
                pad[x + a, pl.ds(m * rows_y + b, rows_y)].reshape(rows_y * cz, 128)
                for a in range(3)
                for b in range(3)
            ],
            axis=1,
        )
        rhs = jnp.concatenate(
            [jnp.concatenate([cw_v[ab * 3 + d] for d in range(3)], axis=1) for ab in range(9)], axis=0
        )
        acc = jnp.dot(lhs, rhs, preferred_element_type=F32)
        z = lax.broadcasted_iota(jnp.int32, (rows_y * cz, 128), 0) % cz
        low = pltpu.roll(acc[:, 0:128], 1, axis=0)
        high = pltpu.roll(acc[:, 256:384], rows_y * cz - 1, axis=0)
        total = acc[:, 128:256] + jnp.where(z == 0, 0.0, low) + jnp.where(z == cz - 1, 0.0, high)
        start = pl.multiple_of(m * rows_y * cz, rows_y * cz)
        conv[x, pl.ds(start, rows_y * cz), :] = total + bias[...]

    def conv_blocks(count, place):
        def step(i, carry):
            conv_block(*place(i))
            return carry

        lax.fori_loop(0, count, step, 0)

    conv_blocks(4, lambda i: (1 + i // 2, 1 + i % 2))

    pl.semaphore_wait(wave.at[0], ly - 1)
    pl.semaphore_signal(wave.at[1], inc=1, **peer(to_x[0] + to_z[1] + to_y[0], gy))

    def arrived(ref, recv_sem):
        pltpu.make_async_remote_copy(
            src_ref=ref, dst_ref=ref, send_sem=sent, recv_sem=recv_sem, **peer(gx, gy)
        ).wait_recv()

    arrived(rcv2, ring_r)

    rows = slice((nz - 1) * 64, nz * 64)
    lane = lax.broadcasted_iota(jnp.int32, (32, 128), 1)
    for x in range(cx):
        cols = slice(x * 128, x * 128 + 128)
        band = own1[rows, cols] + rcv1[rows, cols].astype(F32)
        for d in range(nz - 1):
            band = band + rcv2[d, :, cols].astype(F32)
        re, im = band[:32], band[32:]
        stage[pl.ds(x, 32, stride=8), :] = jnp.where(lane < 64, re, pltpu.roll(im, 64, axis=1))
        stage[pl.ds(4 + x, 32, stride=8), :] = jnp.where(lane < 64, pltpu.roll(re, 64, axis=1), im)
    snda[...] = stage[...].astype(BF).reshape(nx, 4, 128)

    pl.semaphore_wait(wave.at[1], 1)

    hops = lambda i, n: min(i, n - i)
    order = [(x, z, y) for x in range(lx) for z in range(lz) for y in range(ly)]
    order.sort(key=lambda o: -(hops(o[0], lx) + hops(o[1], lz) + hops(o[2], ly)))

    def exchange(src, dst, number):
        for x, z, y in order[:-1]:
            to = to_x[x] + to_z[z] + to_y[y]
            send(src.at[to], dst.at[gx], a2a_r.at[number], peer(to, gy))

    def wait_exchange(dst, number):
        arrived(dst.at[pl.ds(0, nx - 1)], a2a_r.at[number])

    exchange(snda, rcva, 0)
    rcva[gx] = snda[gx]

    for n in (6, 7):
        start_halo(n, jnp.logical_not(near[n]))

    low_near, high_near = near[7], near[6]
    wait_halo(6, low_near)
    wait_halo(7, high_near)
    conv_blocks(jnp.where(low_near, 2, 0), lambda i: (0, 1 + i))
    conv_blocks(jnp.where(high_near, 2, 0), lambda i: (cx - 1, 1 + i))
    load_weight.wait()
    load_x.wait()

    wait_exchange(rcva, 0)

    g = rcva[...].reshape(nx * 4, 128)
    full = nx * cx
    table = jnp.concatenate([x_v[2 * full : 2 * full + 128], x_v[2 * full + 128 :]], axis=1)
    p = jnp.dot(table, g, preferred_element_type=F32)
    lane = lax.broadcasted_iota(jnp.int32, (MX, 128), 1)
    sign = jnp.where(lane < 64, 1.0, -1.0).astype(F32)
    spec = p[:MX] + sign * pltpu.roll(p[MX:], 64, axis=1)

    row0 = spec * sign
    row1 = pltpu.roll(spec, 64, axis=1)
    sub = lax.broadcasted_iota(jnp.int32, (16, 128), 0) % 8
    mixed = []
    for blk in range(MX // 8):
        rows16 = jnp.concatenate([row0[blk * 8 : blk * 8 + 8], row1[blk * 8 : blk * 8 + 8]], axis=0)
        lhs = jnp.concatenate(
            [jnp.where(sub == i, rows16, 0.0).astype(BF) for i in range(8)], axis=1
        )
        rhs = w_v[blk * 8 : blk * 8 + 8].reshape(8 * 128, 128)
        mixed.append(jnp.dot(lhs, rhs, preferred_element_type=F32))
    mixed = jnp.concatenate(mixed, axis=0).astype(BF)

    back = jnp.dot(x_v[: 2 * full, :], mixed, preferred_element_type=F32)
    sndb[...] = back.astype(BF).reshape(nx, 8, 128)

    exchange(sndb, rcvb, 1)
    rcvb[gx] = sndb[gx]

    for n in range(6):
        start_halo(n)

    wait_halo(6, jnp.logical_not(low_near))
    wait_halo(7, jnp.logical_not(high_near))

    conv_blocks(jnp.where(low_near, 0, 2), lambda i: (0, 1 + i))
    conv_blocks(jnp.where(high_near, 0, 2), lambda i: (cx - 1, 1 + i))

    wait_exchange(rcvb, 1)

    both = rcvb[...].astype(F32).reshape(nx // 2, 2, 8, 128)
    stage[...] = (both[:, 0] + both[:, 1]).reshape(nx // 2 * 8, 128)
    slot = core * nz + zh
    for q in range(2):
        for x in range(cx):
            coef[q, slot, :, x * 128 : x * 128 + 128] = stage[
                pl.ds(q * 4 + x, 32, stride=8), :
            ].astype(BF)

    gathers = [
        send(
            coef.at[:, slot], coef.at[:, slot], ag_r.at[d - 1],
            peer(gx, ((zh + d) % nz) * 2 + core),
        )
        for d in order_z[:-1]
    ]

    def pass_on(d):
        there = coef.at[:, core * nz + (zh - d + nz) % nz]
        send(there, there, fw_r, peer(gx, partner))

    pass_on(0)

    for n in range(6):
        wait_halo(n)

    conv_blocks(8, lambda i: (i % cx, 3 * (i // cx)))

    for n in (1, 2, 0):
        gathers[n].wait_recv()
        pass_on(order_z[n])

    arrived(coef.at[:, pl.ds((1 - core) * nz, nz)], fw_r)

    root = math.sqrt(2.0 / math.pi)
    parts = 4

    def finish(i, carry):
        size = cells // parts
        rows = pl.ds(pl.multiple_of(i * size, size), size)
        lhs = brot[rows, :]
        for xp in range(cx // 2):
            rhs = coef[:, :, :, xp * 256 : xp * 256 + 256].reshape(2 * MY * MZ, 256)
            acc = jnp.dot(lhs, rhs, preferred_element_type=F32)
            for x in range(2):
                v = acc[:, x * 128 : x * 128 + 128] + conv[2 * xp + x, rows, :]
                t = jnp.tanh(v * (root + (root * 0.044715) * (v * v)))
                v = 0.5 * v
                out[2 * xp + x, rows, :] = (v + v * t).astype(BF)
        return carry

    lax.fori_loop(0, parts, finish, 0, unroll=True)

    pltpu.make_async_remote_copy(
        src_ref=sizes, dst_ref=sizes, send_sem=sent, recv_sem=fw_r, **peer(gx, gy)
    ).wait_send()
    for n in range(8):
        @pl.when(inside_grid(n, 1))
        def _(n=n):
            halo(n).wait_send()


def body(consts, nx, ny, flow_field, spectral_weight, conv_weight, channel_bias):
    cells_x, cells_y, cells_z, channels = flow_field.shape
    cells = cells_y * cells_z
    nz = ny // 2
    modes = 2 * MY * MZ
    v = pltpu.VMEM
    dma = pltpu.SemaphoreType.DMA
    vmem = pl.BlockSpec(memory_space=pltpu.VMEM)
    band = 64 * cells_x // 4
    sent_kib = band * (nz + 2 * (nz - 1) + nz) + 3 * (nx - 1)
    out = pl.pallas_call(
        functools.partial(kernel, nx, ny),
        out_shape=pltpu.VMEM((cells_x, cells, channels), BF),
        in_specs=[ANY] * 7,
        out_specs=vmem,
        scratch_shapes=[
            v((cells_x + 2, cells_y + 2, cells_z, channels), BF),
            v((MX, 128, 128), BF),
            v((27, 128, 128), BF),
            v((1, channels), F32),
            v((modes, cells), BF),
            v((cells, modes), BF),
            v((2 * nx * cells_x + 4 * MX, 2 * MX), BF),
            v((cells, modes), BF),
            v((modes // 2, cells_x * 128), BF),
            v((modes // 2, cells_x * 128), F32),
            v((modes // 2, cells_x * 128), BF),
            v((modes // 2, cells_x * 128), BF),
            v((nz - 1, 64, cells_x * 128), BF),
            v((256, 128), F32),
            v((nx, 4, 128), BF),
            v((nx, 4, 128), BF),
            v((nx, 8, 128), BF),
            v((nx, 8, 128), BF),
            v((2, ny, 32, cells_x * 128), BF),
            v((cells_x, cells, 128), F32),
            v((sent_kib, 4, 128), BF),
            dma((6,)),
            pltpu.SemaphoreType.REGULAR((2,)),
            dma,
            dma((8,)),
            dma((8,)),
            dma((2,)),
            dma,
            dma((2,)),
            dma((nz - 1,)),
            dma,
        ],
        compiler_params=pltpu.CompilerParams(collective_id=0, has_side_effects=True),
        name="layer",
    )(
        flow_field,
        spectral_weight.reshape(MX, 128, 128),
        conv_weight.reshape(27, 128, 128),
        channel_bias.reshape(1, channels),
        *consts,
    )
    return out.reshape(cells_x, cells_y, cells_z, channels)


def solution(mesh):
    nx, ny = mesh.shape["gx"], mesh.shape["gy"]
    consts = tables(nx, ny, 4, 16, 64)

    def layer(*args):
        return body(tuple(jnp.asarray(c) for c in consts), nx, ny, *args)

    placed = (P("gx", "gy", None, None), P(("gy", "gx"), None, None, None, None), P(), P())
    return jax.shard_map(
        layer, mesh=mesh, in_specs=placed, out_specs=P("gx", "gy", None, None), check_vma=False
    )
```

```python
import functools
import math

import jax
import jax.numpy as jnp
import numpy as np
from jax import lax
from jax.experimental import pallas as pl
from jax.experimental.pallas import tpu as pltpu
from jax.sharding import PartitionSpec as P

MX = 64
MY = 16
MZ = 16
MESH = pl.DeviceIdType.MESH
ANY = pl.BlockSpec(memory_space=pl.ANY)
BF = jnp.bfloat16
F32 = jnp.float32


def signed(count):
    position = np.arange(count)
    return np.where(position < count // 2, position, position - count)


def angles(first, second, length):
    return (np.multiply.outer(first, second) % length) * (2.0 * math.pi / length)


def rounded(values):
    return np.asarray(values, dtype=BF)


def tables(count_x, count_y, cells_x, cells_y, cells_z):
    full_x, full_y = count_x * cells_x, count_y * cells_y
    half = count_y // 2
    theta = angles(np.arange(cells_z), np.arange(MZ), cells_z)
    forward = [
        rounded(f(theta) * s * cells_z**-0.5).astype(np.float64) for f, s in ((np.cos, 1), (np.sin, -1))
    ]
    backward = [
        rounded(f(theta) * s * MZ**-0.5).astype(np.float64) for f, s in ((np.cos, 1), (np.sin, -1))
    ]
    phi = angles(signed(MY), np.arange(cells_y), full_y)
    cos, sin = np.cos(phi), np.sin(phi)
    outer = lambda a, b: np.einsum("jy,zk->jkyz", a, b)
    a_re = (outer(cos, forward[0]) + outer(sin, forward[1])) * full_y**-0.5
    a_im = (outer(cos, forward[1]) - outer(sin, forward[0])) * full_y**-0.5
    b_re = (outer(cos, backward[0]) + outer(sin, backward[1])) * MY**-0.5
    b_im = (outer(cos, backward[1]) - outer(sin, backward[0])) * MY**-0.5
    band = MY // count_y
    cells = cells_y * cells_z
    split = (half, 2, band, MZ, cells)
    a = np.stack([a_re.reshape(split), a_im.reshape(split)])
    a = a.transpose(2, 1, 0, 3, 4, 5).reshape(2 * MY * MZ, cells)
    b = np.stack([b_re.reshape(split), b_im.reshape(split)])
    b = 0.5 * b.transpose(0, 2, 1, 3, 4, 5).reshape(2 * MY * MZ, cells).T
    theta = angles(signed(MX), np.arange(full_x), full_x)
    t = np.concatenate([np.cos(theta), np.sin(theta)]) * full_x**-0.5
    cos, sin = np.cos(theta.T), np.sin(theta.T)
    ix = np.stack([np.stack([cos, -sin]), np.stack([sin, cos])]) * MX**-0.5
    ix = ix.reshape(2, 2, count_x, cells_x, MX // 8, 8).transpose(2, 0, 3, 4, 1, 5)
    ix = ix.reshape(2 * full_x, 2 * MX)
    x = np.concatenate([ix, t[:, :128], t[:, 128:]])
    return tuple(rounded(v) for v in (a, b, x))


def eighth(t):
    r = math.sqrt(0.5)

    def value(t):
        return jnp.where(
            t == 0,
            1.0,
            jnp.where(
                t == 4,
                -1.0,
                jnp.where((t == 2) | (t == 6), 0.0, jnp.where((t == 1) | (t == 7), r, -r)),
            ),
        ).astype(F32)

    return value(t), value((t + 6) % 8)


def kernel(
    nx, ny,
    flow, weight, conv_w, bias_hbm, a_hbm, b_hbm, x_hbm,
    out,
    pad, w_v, cw_v, bias, a_v, b_v, x_v, brot,
    snd1, own1, rcv1, snd2, rcv2, stage, snda, rcva, sndb, rcvb, coef, conv, sizes,
    load_sem, wave, sent, halo_s, halo_r, pair_r, ring_r, a2a_r, ag_r, own_r, fw_r,
):
    gx, gy = lax.axis_index("gx"), lax.axis_index("gy")
    zh, core = gy // 2, gy % 2
    nz = ny // 2
    cx = flow.shape[0]
    cy = flow.shape[1]
    cz = flow.shape[2]
    cells = cy * cz
    lx, lz, ly = nx // 16, 2, 8
    at_x, at_z, at_y = gx // 16, (gx // 8) % 2, gx % 8
    to_x = [((at_x + i) % lx) * 16 for i in range(lx)]
    to_z = [((at_z + i) % lz) * 8 for i in range(lz)]
    to_y = [(at_y + i) % ly for i in range(ly)]

    half_rows = nz * 64
    first_rows = pl.ds(pl.multiple_of((1 - core) * half_rows, half_rows), half_rows)
    other_rows = pl.ds(pl.multiple_of(core * half_rows, half_rows), half_rows)

    def load(source, target, number):
        return pltpu.make_async_copy(source, target, load_sem.at[number])

    load_flow = load(flow, pad.at[pl.ds(1, cx), pl.ds(1, cy)], 0)
    load_first = load(a_hbm.at[first_rows], a_v.at[first_rows], 1)
    load_other = load(a_hbm.at[other_rows], a_v.at[other_rows], 2)
    load_back = load(b_hbm, b_v, 0)
    load_conv = load(conv_w, cw_v, 1)
    load_bias = load(bias_hbm, bias, 3)
    load_weight = load(weight, w_v, 4)
    load_x = load(x_hbm, x_v, 5)
    load_first.start()
    for x in range(cx):
        load(flow.at[x], pad.at[1 + x, pl.ds(1, cy)], 0).start()

    barrier = pltpu.get_barrier_semaphore()
    partner = gy + 1 - 2 * core
    beside = (gy + ny - 1 + 2 * core) % ny
    next_x, last_x = (gx + 1) % nx, (gx + nx - 1) % nx

    def peer(x, y):
        return {"device_id": (x, y), "device_id_type": MESH}

    greeted = [(gx, ((zh + d) % nz) * 2 + core) for d in range(1, nz)]
    greeted += [(to_x[0] + to_z[0] + to_y[i], gy) for i in range(1, ly)]
    greeted += [(to_x[i] + to_z[0] + to_y[0], gy) for i in range(1, lx)]
    greeted += [(to_x[0] + to_z[1] + to_y[0], gy)]
    greeted += [(x, y) for y in (partner, beside) for x in (gx, next_x, last_x)]
    greeted += [(next_x, gy), (last_x, gy)]
    for x, y in greeted:
        pl.semaphore_signal(barrier, inc=1, **peer(x, y))

    zero_plane = jnp.zeros((cy + 2, cz, 128), BF)
    zero_row = jnp.zeros((cx + 2, 1, cz, 128), BF)

    @pl.when(gx == 0)
    def _():
        pad[0] = zero_plane

    @pl.when(gx == nx - 1)
    def _():
        pad[cx + 1] = zero_plane

    @pl.when(gy == 0)
    def _():
        pad[:, 0:1] = zero_row

    @pl.when(gy == ny - 1)
    def _():
        pad[:, cy + 1 : cy + 2] = zero_row

    load_first.wait()
    load_flow.wait()
    load_other.start()

    order_z = (2, 1, 3, 0)

    def send(source, target, recv_sem, device):
        copy = pltpu.make_async_remote_copy(
            src_ref=source, dst_ref=target, send_sem=sent, recv_sem=recv_sem, **device
        )
        copy.start()
        return copy

    def forward(half, save):
        targets = [(zh + d) % nz for d in order_z]
        rows = jnp.concatenate(
            [a_v[pl.ds(pl.multiple_of((half * nz + z) * 64, 64), 64), :] for z in targets], axis=0
        )
        spins = [[eighth(((2 * (2 * z + half) + j2) * gy) % 8) for j2 in range(2)] for z in targets]
        for xp in range(cx // 2):
            rhs = jnp.concatenate(
                [pad[1 + 2 * xp + i, 1 : cy + 1].reshape(cells, 128) for i in range(2)], axis=1
            )
            y = jnp.dot(rows, rhs, preferred_element_type=F32)
            for n in range(nz):
                for j2 in range(2):
                    c, s = spins[n][j2]
                    r0 = n * 64 + j2 * 16
                    re, im = y[r0 : r0 + 16], y[r0 + 32 : r0 + 48]
                    save(r0, xp, c * re + s * im)
                    save(r0 + 32, xp, c * im - s * re)

    def save_send(r0, xp, v):
        snd1[r0 : r0 + 16, xp * 256 : xp * 256 + 256] = v.astype(BF)

    def save_own(r0, xp, v):
        own1[r0 : r0 + 16, xp * 256 : xp * 256 + 256] = v

    forward(1 - core, save_send)
    for item in (load_back, load_conv, load_bias, load_weight, load_x):
        item.start()

    pl.semaphore_wait(barrier, len(greeted))

    pair_rows = (pl.ds(0, 64), pl.ds(64, (nz - 1) * 64))
    pairs = [
        send(snd1.at[rows], rcv1.at[rows], pair_r.at[n], peer(gx, partner))
        for n, rows in enumerate(pair_rows)
    ]
    for i in range(1, ly):
        pl.semaphore_signal(wave.at[0], inc=1, **peer(to_x[0] + to_z[0] + to_y[i], gy))

    inner_x, inner_y = pl.ds(1, cx), pl.ds(1, cy)

    def place(step, count, inner, send):
        if step == 0:
            return inner
        edge = (count if step > 0 else 1) if send else (0 if step > 0 else count + 1)
        return pl.ds(edge, 1)

    steps = ((0, 1), (0, -1), (1, 1), (1, -1), (-1, 1), (-1, -1), (1, 0), (-1, 0))

    def halo(n):
        dx, dy = steps[n]
        return pltpu.make_async_remote_copy(
            src_ref=pad.at[place(dx, cx, inner_x, True), place(dy, cy, inner_y, True)],
            dst_ref=pad.at[place(dx, cx, inner_x, False), place(dy, cy, inner_y, False)],
            send_sem=halo_s.at[n], recv_sem=halo_r.at[n],
            **peer((gx + dx + nx) % nx, (gy + dy + ny) % ny),
        )

    def inside_grid(n, sign):
        dx, dy = steps[n]
        x, y = gx + sign * dx, gy + sign * dy
        return (x >= 0) & (x < nx) & (y >= 0) & (y < ny)

    def start_halo(n, condition=True):
        @pl.when(inside_grid(n, 1) & condition)
        def _():
            halo(n).start()

    def wait_halo(n, condition=True):
        @pl.when(inside_grid(n, -1) & condition)
        def _():
            halo(n).wait_recv()

    near = {6: at_y < ly - 1, 7: at_y > 0}
    for n in (6, 7):
        start_halo(n, near[n])

    load_other.wait()
    forward(core, save_own)

    for n, d in enumerate(order_z[:-1]):
        rows = slice(n * 64, n * 64 + 64)
        if n < 2:
            pairs[n].wait_recv()
        snd2[rows, :] = (own1[rows, :] + rcv1[rows, :].astype(F32)).astype(BF)
        send(snd2.at[rows], rcv2.at[n], ring_r, peer(gx, ((zh + d) % nz) * 2 + core))

    load_back.wait()
    lanes = lax.broadcasted_iota(jnp.int32, (1, MY * MZ), 1)
    mode = 2 * (2 * ((lanes // 32) % nz) + lanes // (32 * nz)) + (lanes // 16) % 2
    spin_c, spin_s = eighth((mode * gy) % 8)

    def rotate(i, carry):
        rows = pl.ds(pl.multiple_of(i * 64, 64), 64)
        re = b_v[rows, 0:256].astype(F32)
        im = b_v[rows, 256:512].astype(F32)
        brot[rows, 0:256] = (spin_c * re + spin_s * im).astype(BF)
        brot[rows, 256:512] = (spin_c * im - spin_s * re).astype(BF)
        return carry

    lax.fori_loop(0, cells // 64, rotate, 0)
    load_conv.wait()
    load_bias.wait()

    rows_y = cy // 4

    def conv_block(x, m):
        lhs = jnp.concatenate(
            [
                pad[x + a, pl.ds(m * rows_y + b, rows_y)].reshape(rows_y * cz, 128)
                for a in range(3)
                for b in range(3)
            ],
            axis=1,
        )
        rhs = jnp.concatenate(
            [jnp.concatenate([cw_v[ab * 3 + d] for d in range(3)], axis=1) for ab in range(9)], axis=0
        )
        acc = jnp.dot(lhs, rhs, preferred_element_type=F32)
        z = lax.broadcasted_iota(jnp.int32, (rows_y * cz, 128), 0) % cz
        low = pltpu.roll(acc[:, 0:128], 1, axis=0)
        high = pltpu.roll(acc[:, 256:384], rows_y * cz - 1, axis=0)
        total = acc[:, 128:256] + jnp.where(z == 0, 0.0, low) + jnp.where(z == cz - 1, 0.0, high)
        start = pl.multiple_of(m * rows_y * cz, rows_y * cz)
        conv[x, pl.ds(start, rows_y * cz), :] = 0.5 * (total + bias[...])

    def conv_blocks(count, place):
        def step(i, carry):
            conv_block(*place(i))
            return carry

        lax.fori_loop(0, count, step, 0)

    conv_blocks(4, lambda i: (1 + i // 2, 1 + i % 2))

    pl.semaphore_wait(wave.at[0], ly - 1)
    pl.semaphore_signal(wave.at[1], inc=1, **peer(to_x[0] + to_z[1] + to_y[0], gy))

    def arrived(ref, recv_sem):
        pltpu.make_async_remote_copy(
            src_ref=ref, dst_ref=ref, send_sem=sent, recv_sem=recv_sem, **peer(gx, gy)
        ).wait_recv()

    arrived(rcv2, ring_r)

    rows = slice((nz - 1) * 64, nz * 64)
    lane = lax.broadcasted_iota(jnp.int32, (32, 128), 1)
    for x in range(cx):
        cols = slice(x * 128, x * 128 + 128)
        band = own1[rows, cols] + rcv1[rows, cols].astype(F32)
        for d in range(nz - 1):
            band = band + rcv2[d, :, cols].astype(F32)
        re, im = band[:32], band[32:]
        stage[pl.ds(x, 32, stride=8), :] = jnp.where(lane < 64, re, pltpu.roll(im, 64, axis=1))
        stage[pl.ds(4 + x, 32, stride=8), :] = jnp.where(lane < 64, pltpu.roll(re, 64, axis=1), im)
    snda[...] = stage[...].astype(BF).reshape(nx, 4, 128)

    pl.semaphore_wait(wave.at[1], 1)

    hops = lambda i, n: min(i, n - i)
    order = [(x, z, y) for x in range(lx) for z in range(lz) for y in range(ly)]
    order.sort(key=lambda o: -(hops(o[0], lx) + hops(o[1], lz) + hops(o[2], ly)))

    def exchange(src, dst, number):
        for x, z, y in order[:-1]:
            to = to_x[x] + to_z[z] + to_y[y]
            send(src.at[to], dst.at[gx], a2a_r.at[number], peer(to, gy))

    def wait_exchange(dst, number):
        arrived(dst.at[pl.ds(0, nx - 1)], a2a_r.at[number])

    exchange(snda, rcva, 0)
    rcva[gx] = snda[gx]

    for n in (6, 7):
        start_halo(n, jnp.logical_not(near[n]))

    low_near, high_near = near[7], near[6]
    wait_halo(6, low_near)
    wait_halo(7, high_near)
    conv_blocks(jnp.where(low_near, 2, 0), lambda i: (0, 1 + i))
    conv_blocks(jnp.where(high_near, 2, 0), lambda i: (cx - 1, 1 + i))
    load_weight.wait()
    load_x.wait()

    wait_exchange(rcva, 0)

    g = rcva[...].reshape(nx * 4, 128)
    full = nx * cx
    table = jnp.concatenate([x_v[2 * full : 2 * full + 128], x_v[2 * full + 128 :]], axis=1)
    p = jnp.dot(table, g, preferred_element_type=F32)
    lane = lax.broadcasted_iota(jnp.int32, (MX, 128), 1)
    sign = jnp.where(lane < 64, 1.0, -1.0).astype(F32)
    spec = p[:MX] + sign * pltpu.roll(p[MX:], 64, axis=1)

    row0 = spec * sign
    row1 = pltpu.roll(spec, 64, axis=1)
    sub = lax.broadcasted_iota(jnp.int32, (16, 128), 0) % 8
    mixed = []
    for blk in range(MX // 8):
        rows16 = jnp.concatenate([row0[blk * 8 : blk * 8 + 8], row1[blk * 8 : blk * 8 + 8]], axis=0)
        lhs = jnp.concatenate(
            [jnp.where(sub == i, rows16, 0.0).astype(BF) for i in range(8)], axis=1
        )
        rhs = w_v[blk * 8 : blk * 8 + 8].reshape(8 * 128, 128)
        mixed.append(jnp.dot(lhs, rhs, preferred_element_type=F32))
    mixed = jnp.concatenate(mixed, axis=0).astype(BF)

    back = jnp.dot(x_v[: 2 * full, :], mixed, preferred_element_type=F32)
    sndb[...] = back.astype(BF).reshape(nx, 8, 128)

    exchange(sndb, rcvb, 1)
    rcvb[gx] = sndb[gx]

    for n in range(6):
        start_halo(n)

    wait_halo(6, jnp.logical_not(low_near))
    wait_halo(7, jnp.logical_not(high_near))

    conv_blocks(jnp.where(low_near, 0, 2), lambda i: (0, 1 + i))
    conv_blocks(jnp.where(high_near, 0, 2), lambda i: (cx - 1, 1 + i))

    wait_exchange(rcvb, 1)

    both = rcvb[...].astype(F32).reshape(nx // 2, 2, 8, 128)
    stage[...] = (both[:, 0] + both[:, 1]).reshape(nx // 2 * 8, 128)
    slot = core * nz + zh
    for q in range(2):
        for x in range(cx):
            coef[q, slot, :, x * 128 : x * 128 + 128] = stage[
                pl.ds(q * 4 + x, 32, stride=8), :
            ].astype(BF)

    chunk = 16 * cx

    def band(owner, d):
        return coef.at[:, owner * nz + (zh - d + nz) % nz]

    def along_z(piece, number, d):
        send(piece, piece, ag_r.at[number], peer(gx, ((zh + d) % nz) * 2 + core))

    def pass_on(piece, recv_sem):
        send(piece, piece, recv_sem, peer(gx, partner))

    @pl.when(core == 0)
    def _():
        pass_on(band(0, 0), own_r)
        for d in (1, 3):
            along_z(band(0, 0), d - 1, d)

    @pl.when(core == 1)
    def _():
        for d in (2, 1, 3):
            along_z(band(1, 0), d - 1, d)
        pass_on(band(1, 0), fw_r)

    for n in range(6):
        wait_halo(n)

    conv_blocks(3, lambda i: (i, 0))

    @pl.when(core == 1)
    def _():
        arrived(band(0, 0), own_r)
        along_z(band(0, 0), 3, 2)

    conv_blocks(5, lambda i: ((i + 3) % cx, 3 * ((i + 3) // cx)))

    @pl.when(core == 0)
    def _():
        for d in (1, 3):
            arrived(band(0, d), ag_r.at[d - 1])
            pass_on(band(0, d), fw_r)

    @pl.when(core == 1)
    def _():
        for d in (1, 3, 2):
            arrived(band(1, d), ag_r.at[d - 1])
            pass_on(band(1, d), fw_r)
        arrived(band(0, 2), ag_r.at[3])
        pass_on(band(0, 2), fw_r)

    @pl.when(core == 0)
    def _():
        arrived(sizes.at[pl.ds(0, 5 * chunk)], fw_r)

    @pl.when(core == 1)
    def _():
        arrived(sizes.at[pl.ds(0, 2 * chunk)], fw_r)

    root = math.sqrt(2.0 / math.pi)
    parts = 4

    def finish(i, carry):
        size = cells // parts
        rows = pl.ds(pl.multiple_of(i * size, size), size)
        lhs = brot[rows, :]
        for xp in range(cx // 2):
            rhs = coef[:, :, :, xp * 256 : xp * 256 + 256].reshape(2 * MY * MZ, 256)
            acc = jnp.dot(lhs, rhs, preferred_element_type=F32)
            for x in range(2):
                v = acc[:, x * 128 : x * 128 + 128] + conv[2 * xp + x, rows, :]
                t = jnp.tanh(v * (2.0 * root + (8.0 * 0.044715 * root) * (v * v)))
                out[2 * xp + x, rows, :] = (v + v * t).astype(BF)
        return carry

    lax.fori_loop(0, parts, finish, 0, unroll=True)

    def all_sent(count):
        ref = sizes.at[pl.ds(0, count)]
        pltpu.make_async_remote_copy(
            src_ref=ref, dst_ref=ref, send_sem=sent, recv_sem=fw_r, **peer(gx, gy)
        ).wait_send()

    pl.when(core == 0)(lambda: all_sent(sizes.shape[0] - 4 * chunk))
    pl.when(core == 1)(lambda: all_sent(sizes.shape[0]))
    for n in range(8):
        @pl.when(inside_grid(n, 1))
        def _(n=n):
            halo(n).wait_send()


def body(consts, nx, ny, flow_field, spectral_weight, conv_weight, channel_bias):
    cells_x, cells_y, cells_z, channels = flow_field.shape
    cells = cells_y * cells_z
    nz = ny // 2
    modes = 2 * MY * MZ
    v = pltpu.VMEM
    dma = pltpu.SemaphoreType.DMA
    vmem = pl.BlockSpec(memory_space=pltpu.VMEM)
    band = 64 * cells_x // 4
    sent_kib = band * (nz + (nz - 1) + 9) + 3 * (nx - 1)
    out = pl.pallas_call(
        functools.partial(kernel, nx, ny),
        out_shape=pltpu.VMEM((cells_x, cells, channels), BF),
        in_specs=[ANY] * 7,
        out_specs=vmem,
        scratch_shapes=[
            v((cells_x + 2, cells_y + 2, cells_z, channels), BF),
            v((MX, 128, 128), BF),
            v((27, 128, 128), BF),
            v((1, channels), F32),
            v((modes, cells), BF),
            v((cells, modes), BF),
            v((2 * nx * cells_x + 4 * MX, 2 * MX), BF),
            v((cells, modes), BF),
            v((modes // 2, cells_x * 128), BF),
            v((modes // 2, cells_x * 128), F32),
            v((modes // 2, cells_x * 128), BF),
            v((modes // 2, cells_x * 128), BF),
            v((nz - 1, 64, cells_x * 128), BF),
            v((256, 128), F32),
            v((nx, 4, 128), BF),
            v((nx, 4, 128), BF),
            v((nx, 8, 128), BF),
            v((nx, 8, 128), BF),
            v((2, ny, 32, cells_x * 128), BF),
            v((cells_x, cells, 128), F32),
            v((sent_kib, 4, 128), BF),
            dma((6,)),
            pltpu.SemaphoreType.REGULAR((2,)),
            dma,
            dma((8,)),
            dma((8,)),
            dma((2,)),
            dma,
            dma((2,)),
            dma((nz,)),
            dma,
            dma,
        ],
        compiler_params=pltpu.CompilerParams(collective_id=0, has_side_effects=True),
        name="layer",
    )(
        flow_field,
        spectral_weight.reshape(MX, 128, 128),
        conv_weight.reshape(27, 128, 128),
        channel_bias.reshape(1, channels),
        *consts,
    )
    return out.reshape(cells_x, cells_y, cells_z, channels)


def solution(mesh):
    nx, ny = mesh.shape["gx"], mesh.shape["gy"]
    consts = tables(nx, ny, 4, 16, 64)

    def layer(*args):
        return body(tuple(jnp.asarray(c) for c in consts), nx, ny, *args)

    placed = (P("gx", "gy", None, None), P(("gy", "gx"), None, None, None, None), P(), P())
    return jax.shard_map(
        layer, mesh=mesh, in_specs=placed, out_specs=P("gx", "gy", None, None), check_vma=False
    )
```

```python
import functools
import math

import jax
import jax.numpy as jnp
import numpy as np
from jax import lax
from jax.experimental import pallas as pl
from jax.experimental.pallas import tpu as pltpu
from jax.sharding import PartitionSpec as P

MX = 64
MY = 16
MZ = 16
MESH = pl.DeviceIdType.MESH
ANY = pl.BlockSpec(memory_space=pl.ANY)
BF = jnp.bfloat16
F32 = jnp.float32


def signed(count):
    position = np.arange(count)
    return np.where(position < count // 2, position, position - count)


def angles(first, second, length):
    return (np.multiply.outer(first, second) % length) * (2.0 * math.pi / length)


def rounded(values):
    return np.asarray(values, dtype=BF)


def tables(count_x, count_y, cells_x, cells_y, cells_z):
    full_x, full_y = count_x * cells_x, count_y * cells_y
    half = count_y // 2
    theta = angles(np.arange(cells_z), np.arange(MZ), cells_z)
    forward = [
        rounded(f(theta) * s * cells_z**-0.5).astype(np.float64) for f, s in ((np.cos, 1), (np.sin, -1))
    ]
    backward = [
        rounded(f(theta) * s * MZ**-0.5).astype(np.float64) for f, s in ((np.cos, 1), (np.sin, -1))
    ]
    phi = angles(signed(MY), np.arange(cells_y), full_y)
    cos, sin = np.cos(phi), np.sin(phi)
    outer = lambda a, b: np.einsum("jy,zk->jkyz", a, b)
    a_re = (outer(cos, forward[0]) + outer(sin, forward[1])) * full_y**-0.5
    a_im = (outer(cos, forward[1]) - outer(sin, forward[0])) * full_y**-0.5
    b_re = (outer(cos, backward[0]) + outer(sin, backward[1])) * MY**-0.5
    b_im = (outer(cos, backward[1]) - outer(sin, backward[0])) * MY**-0.5
    band = MY // count_y
    cells = cells_y * cells_z
    split = (half, 2, band, MZ, cells)
    a = np.stack([a_re.reshape(split), a_im.reshape(split)])
    a = a.transpose(2, 1, 0, 3, 4, 5).reshape(2 * MY * MZ, cells)
    b = np.stack([b_re.reshape(split), b_im.reshape(split)])
    b = 0.5 * b.transpose(0, 2, 1, 3, 4, 5).reshape(2 * MY * MZ, cells).T
    theta = angles(signed(MX), np.arange(full_x), full_x)
    t = np.concatenate([np.cos(theta), np.sin(theta)]) * full_x**-0.5
    cos, sin = np.cos(theta.T), np.sin(theta.T)
    ix = np.stack([np.stack([cos, -sin]), np.stack([sin, cos])]) * MX**-0.5
    ix = ix.reshape(2, 2, count_x, cells_x, MX // 8, 8).transpose(2, 0, 3, 4, 1, 5)
    ix = ix.reshape(2 * full_x, 2 * MX)
    x = np.concatenate([ix, t[:, :128], t[:, 128:]])
    return tuple(rounded(v) for v in (a, b, x))


def eighth(t):
    r = math.sqrt(0.5)

    def value(t):
        return jnp.where(
            t == 0,
            1.0,
            jnp.where(
                t == 4,
                -1.0,
                jnp.where((t == 2) | (t == 6), 0.0, jnp.where((t == 1) | (t == 7), r, -r)),
            ),
        ).astype(F32)

    return value(t), value((t + 6) % 8)


def kernel(
    nx, ny,
    flow, weight, conv_w, bias_hbm, a_hbm, b_hbm, x_hbm,
    out,
    pad, w_v, cw_v, bias, a_v, b_v, x_v, brot,
    snd1, own1, rcv1, snd2, rcv2, stage, snda, rcva, sndb, rcvb, coef, conv, sizes,
    load_sem, wave, sent, halo_s, halo_r, pair_r, ring_r, a2a_r, ag_r, own_r, fw_r,
):
    gx, gy = lax.axis_index("gx"), lax.axis_index("gy")
    zh, core = gy // 2, gy % 2
    nz = ny // 2
    cx = flow.shape[0]
    cy = flow.shape[1]
    cz = flow.shape[2]
    cells = cy * cz
    lx, lz, ly = nx // 16, 2, 8
    at_x, at_z, at_y = gx // 16, (gx // 8) % 2, gx % 8
    to_x = [((at_x + i) % lx) * 16 for i in range(lx)]
    to_z = [((at_z + i) % lz) * 8 for i in range(lz)]
    to_y = [(at_y + i) % ly for i in range(ly)]

    half_rows = nz * 64
    first_rows = pl.ds(pl.multiple_of((1 - core) * half_rows, half_rows), half_rows)
    other_rows = pl.ds(pl.multiple_of(core * half_rows, half_rows), half_rows)

    def load(source, target, number):
        return pltpu.make_async_copy(source, target, load_sem.at[number])

    load_flow = load(flow, pad.at[pl.ds(1, cx), pl.ds(1, cy)], 0)
    load_first = load(a_hbm.at[first_rows], a_v.at[first_rows], 1)
    load_other = load(a_hbm.at[other_rows], a_v.at[other_rows], 2)
    load_back = load(b_hbm, b_v, 0)
    load_conv = load(conv_w, cw_v, 1)
    load_bias = load(bias_hbm, bias, 3)
    load_weight = load(weight, w_v, 4)
    load_x = load(x_hbm, x_v, 5)
    load_first.start()
    for x in range(cx):
        load(flow.at[x], pad.at[1 + x, pl.ds(1, cy)], 0).start()

    barrier = pltpu.get_barrier_semaphore()
    partner = gy + 1 - 2 * core
    beside = (gy + ny - 1 + 2 * core) % ny
    next_x, last_x = (gx + 1) % nx, (gx + nx - 1) % nx

    def peer(x, y):
        return {"device_id": (x, y), "device_id_type": MESH}

    greeted = [(gx, ((zh + d) % nz) * 2 + core) for d in range(1, nz)]
    greeted += [(to_x[0] + to_z[0] + to_y[i], gy) for i in range(1, ly)]
    greeted += [(to_x[i] + to_z[0] + to_y[0], gy) for i in range(1, lx)]
    greeted += [(to_x[0] + to_z[1] + to_y[0], gy)]
    greeted += [(x, y) for y in (partner, beside) for x in (gx, next_x, last_x)]
    greeted += [(next_x, gy), (last_x, gy)]
    for x, y in greeted:
        pl.semaphore_signal(barrier, inc=1, **peer(x, y))

    zero_plane = jnp.zeros((cy + 2, cz, 128), BF)
    zero_row = jnp.zeros((cx + 2, 1, cz, 128), BF)

    @pl.when(gx == 0)
    def _():
        pad[0] = zero_plane

    @pl.when(gx == nx - 1)
    def _():
        pad[cx + 1] = zero_plane

    @pl.when(gy == 0)
    def _():
        pad[:, 0:1] = zero_row

    @pl.when(gy == ny - 1)
    def _():
        pad[:, cy + 1 : cy + 2] = zero_row

    load_first.wait()
    load_flow.wait()
    load_other.start()

    order_z = (2, 1, 3, 0)

    def send(source, target, recv_sem, device):
        copy = pltpu.make_async_remote_copy(
            src_ref=source, dst_ref=target, send_sem=sent, recv_sem=recv_sem, **device
        )
        copy.start()
        return copy

    def forward(half, save):
        targets = [(zh + d) % nz for d in order_z]
        rows = jnp.concatenate(
            [a_v[pl.ds(pl.multiple_of((half * nz + z) * 64, 64), 64), :] for z in targets], axis=0
        )
        spins = [[eighth(((2 * (2 * z + half) + j2) * gy) % 8) for j2 in range(2)] for z in targets]
        for xp in range(cx // 2):
            rhs = jnp.concatenate(
                [pad[1 + 2 * xp + i, 1 : cy + 1].reshape(cells, 128) for i in range(2)], axis=1
            )
            y = jnp.dot(rows, rhs, preferred_element_type=F32)
            for n in range(nz):
                for j2 in range(2):
                    c, s = spins[n][j2]
                    r0 = n * 64 + j2 * 16
                    re, im = y[r0 : r0 + 16], y[r0 + 32 : r0 + 48]
                    save(r0, xp, c * re + s * im)
                    save(r0 + 32, xp, c * im - s * re)

    def save_send(r0, xp, v):
        snd1[r0 : r0 + 16, xp * 256 : xp * 256 + 256] = v.astype(BF)

    def save_own(r0, xp, v):
        own1[r0 : r0 + 16, xp * 256 : xp * 256 + 256] = v

    forward(1 - core, save_send)
    for item in (load_back, load_conv, load_bias, load_weight, load_x):
        item.start()

    pl.semaphore_wait(barrier, len(greeted))

    pair_rows = (pl.ds(0, 64), pl.ds(64, (nz - 1) * 64))
    pairs = [
        send(snd1.at[rows], rcv1.at[rows], pair_r.at[n], peer(gx, partner))
        for n, rows in enumerate(pair_rows)
    ]
    for i in range(1, ly):
        pl.semaphore_signal(wave.at[0], inc=1, **peer(to_x[0] + to_z[0] + to_y[i], gy))

    inner_x, inner_y = pl.ds(1, cx), pl.ds(1, cy)

    def place(step, count, inner, send):
        if step == 0:
            return inner
        edge = (count if step > 0 else 1) if send else (0 if step > 0 else count + 1)
        return pl.ds(edge, 1)

    steps = ((0, 1), (0, -1), (1, 1), (1, -1), (-1, 1), (-1, -1), (1, 0), (-1, 0))

    def halo(n):
        dx, dy = steps[n]
        return pltpu.make_async_remote_copy(
            src_ref=pad.at[place(dx, cx, inner_x, True), place(dy, cy, inner_y, True)],
            dst_ref=pad.at[place(dx, cx, inner_x, False), place(dy, cy, inner_y, False)],
            send_sem=halo_s.at[n], recv_sem=halo_r.at[n],
            **peer((gx + dx + nx) % nx, (gy + dy + ny) % ny),
        )

    def inside_grid(n, sign):
        dx, dy = steps[n]
        x, y = gx + sign * dx, gy + sign * dy
        return (x >= 0) & (x < nx) & (y >= 0) & (y < ny)

    def start_halo(n, condition=True):
        @pl.when(inside_grid(n, 1) & condition)
        def _():
            halo(n).start()

    def wait_halo(n, condition=True):
        @pl.when(inside_grid(n, -1) & condition)
        def _():
            halo(n).wait_recv()

    near = {6: at_y < ly - 1, 7: at_y > 0}
    for n in (6, 7):
        start_halo(n, near[n])

    load_other.wait()
    forward(core, save_own)

    for n, d in enumerate(order_z[:-1]):
        rows = slice(n * 64, n * 64 + 64)
        if n < 2:
            pairs[n].wait_recv()
        snd2[rows, :] = (own1[rows, :] + rcv1[rows, :].astype(F32)).astype(BF)
        send(snd2.at[rows], rcv2.at[n], ring_r, peer(gx, ((zh + d) % nz) * 2 + core))

    load_back.wait()
    lanes = lax.broadcasted_iota(jnp.int32, (1, MY * MZ), 1)
    mode = 2 * (2 * ((lanes // 32) % nz) + lanes // (32 * nz)) + (lanes // 16) % 2
    spin_c, spin_s = eighth((mode * gy) % 8)

    def rotate(i, carry):
        rows = pl.ds(pl.multiple_of(i * 64, 64), 64)
        re = b_v[rows, 0:256].astype(F32)
        im = b_v[rows, 256:512].astype(F32)
        brot[rows, 0:256] = (spin_c * re + spin_s * im).astype(BF)
        brot[rows, 256:512] = (spin_c * im - spin_s * re).astype(BF)
        return carry

    lax.fori_loop(0, cells // 64, rotate, 0)
    load_conv.wait()
    load_bias.wait()

    rows_y = cy // 4

    def conv_block(x, m):
        lhs = jnp.concatenate(
            [
                pad[x + a, pl.ds(m * rows_y + b, rows_y)].reshape(rows_y * cz, 128)
                for a in range(3)
                for b in range(3)
            ],
            axis=1,
        )
        rhs = jnp.concatenate(
            [jnp.concatenate([cw_v[ab * 3 + d] for d in range(3)], axis=1) for ab in range(9)], axis=0
        )
        acc = jnp.dot(lhs, rhs, preferred_element_type=F32)
        z = lax.broadcasted_iota(jnp.int32, (rows_y * cz, 128), 0) % cz
        low = pltpu.roll(acc[:, 0:128], 1, axis=0)
        high = pltpu.roll(acc[:, 256:384], rows_y * cz - 1, axis=0)
        total = acc[:, 128:256] + jnp.where(z == 0, 0.0, low) + jnp.where(z == cz - 1, 0.0, high)
        start = pl.multiple_of(m * rows_y * cz, rows_y * cz)
        conv[x, pl.ds(start, rows_y * cz), :] = 0.5 * (total + bias[...])

    def conv_blocks(count, place):
        def step(i, carry):
            conv_block(*place(i))
            return carry

        lax.fori_loop(0, count, step, 0)

    conv_blocks(4, lambda i: (1 + i // 2, 1 + i % 2))

    pl.semaphore_wait(wave.at[0], ly - 1)
    pl.semaphore_signal(wave.at[1], inc=1, **peer(to_x[0] + to_z[1] + to_y[0], gy))

    def arrived(ref, recv_sem):
        pltpu.make_async_remote_copy(
            src_ref=ref, dst_ref=ref, send_sem=sent, recv_sem=recv_sem, **peer(gx, gy)
        ).wait_recv()

    arrived(rcv2, ring_r)

    rows = slice((nz - 1) * 64, nz * 64)
    lane = lax.broadcasted_iota(jnp.int32, (32, 128), 1)
    for x in range(cx):
        cols = slice(x * 128, x * 128 + 128)
        band = own1[rows, cols] + rcv1[rows, cols].astype(F32)
        for d in range(nz - 1):
            band = band + rcv2[d, :, cols].astype(F32)
        re, im = band[:32], band[32:]
        stage[pl.ds(x, 32, stride=8), :] = jnp.where(lane < 64, re, pltpu.roll(im, 64, axis=1))
        stage[pl.ds(4 + x, 32, stride=8), :] = jnp.where(lane < 64, pltpu.roll(re, 64, axis=1), im)
    snda[...] = stage[...].astype(BF).reshape(nx, 4, 128)

    pl.semaphore_wait(wave.at[1], 1)

    hops = lambda i, n: min(i, n - i)
    order = [(x, z, y) for x in range(lx) for z in range(lz) for y in range(ly)]
    order.sort(key=lambda o: -(hops(o[0], lx) + hops(o[1], lz) + hops(o[2], ly)))

    def exchange(src, dst, number):
        for x, z, y in order[:-1]:
            to = to_x[x] + to_z[z] + to_y[y]
            send(src.at[to], dst.at[gx], a2a_r.at[number], peer(to, gy))

    def wait_exchange(dst, number):
        arrived(dst.at[pl.ds(0, nx - 1)], a2a_r.at[number])

    exchange(snda, rcva, 0)
    rcva[gx] = snda[gx]

    for n in (6, 7):
        start_halo(n, jnp.logical_not(near[n]))

    low_near, high_near = near[7], near[6]
    wait_halo(6, low_near)
    wait_halo(7, high_near)
    conv_blocks(jnp.where(low_near, 2, 0), lambda i: (0, 1 + i))
    conv_blocks(jnp.where(high_near, 2, 0), lambda i: (cx - 1, 1 + i))
    load_weight.wait()
    load_x.wait()

    wait_exchange(rcva, 0)

    g = rcva[...].reshape(nx * 4, 128)
    full = nx * cx
    table = jnp.concatenate([x_v[2 * full : 2 * full + 128], x_v[2 * full + 128 :]], axis=1)
    p = jnp.dot(table, g, preferred_element_type=F32)
    lane = lax.broadcasted_iota(jnp.int32, (MX, 128), 1)
    sign = jnp.where(lane < 64, 1.0, -1.0).astype(F32)
    spec = p[:MX] + sign * pltpu.roll(p[MX:], 64, axis=1)

    row0 = spec * sign
    row1 = pltpu.roll(spec, 64, axis=1)
    sub = lax.broadcasted_iota(jnp.int32, (16, 128), 0) % 8
    mixed = []
    for blk in range(MX // 8):
        rows16 = jnp.concatenate([row0[blk * 8 : blk * 8 + 8], row1[blk * 8 : blk * 8 + 8]], axis=0)
        lhs = jnp.concatenate(
            [jnp.where(sub == i, rows16, 0.0).astype(BF) for i in range(8)], axis=1
        )
        rhs = w_v[blk * 8 : blk * 8 + 8].reshape(8 * 128, 128)
        mixed.append(jnp.dot(lhs, rhs, preferred_element_type=F32))
    mixed = jnp.concatenate(mixed, axis=0).astype(BF)

    back = jnp.dot(x_v[: 2 * full, :], mixed, preferred_element_type=F32)
    sndb[...] = back.astype(BF).reshape(nx, 8, 128)

    exchange(sndb, rcvb, 1)
    rcvb[gx] = sndb[gx]

    for n in range(6):
        start_halo(n)

    wait_halo(6, jnp.logical_not(low_near))
    wait_halo(7, jnp.logical_not(high_near))

    conv_blocks(jnp.where(low_near, 0, 2), lambda i: (0, 1 + i))
    conv_blocks(jnp.where(high_near, 0, 2), lambda i: (cx - 1, 1 + i))

    wait_exchange(rcvb, 1)

    both = rcvb[...].astype(F32).reshape(nx // 2, 2, 8, 128)
    stage[...] = (both[:, 0] + both[:, 1]).reshape(nx // 2 * 8, 128)
    slot = core * nz + zh
    for q in range(2):
        for x in range(cx):
            coef[q, slot, :, x * 128 : x * 128 + 128] = stage[
                pl.ds(q * 4 + x, 32, stride=8), :
            ].astype(BF)

    chunk = 16 * cx

    def band(owner, d):
        return coef.at[:, owner * nz + (zh - d + nz) % nz]

    def along_z(piece, number, d):
        send(piece, piece, ag_r.at[number], peer(gx, ((zh + d) % nz) * 2 + core))

    def pass_on(piece, recv_sem):
        send(piece, piece, recv_sem, peer(gx, partner))

    @pl.when(core == 0)
    def _():
        pass_on(band(0, 0), own_r)
        for d in (1, 3):
            along_z(band(0, 0), d - 1, d)

    @pl.when(core == 1)
    def _():
        for d in (2, 1, 3):
            along_z(band(1, 0), d - 1, d)
        pass_on(band(1, 0), fw_r)

    @pl.when(core == 1)
    def _():
        arrived(band(0, 0), own_r)
        along_z(band(0, 0), 3, 2)

    for n in range(6):
        wait_halo(n)

    conv_blocks(8, lambda i: (i % cx, 3 * (i // cx)))

    @pl.when(core == 0)
    def _():
        for d in (1, 3):
            arrived(band(0, d), ag_r.at[d - 1])
            pass_on(band(0, d), fw_r)

    @pl.when(core == 1)
    def _():
        for d in (1, 3, 2):
            arrived(band(1, d), ag_r.at[d - 1])
            pass_on(band(1, d), fw_r)
        arrived(band(0, 2), ag_r.at[3])
        pass_on(band(0, 2), fw_r)

    @pl.when(core == 0)
    def _():
        arrived(sizes.at[pl.ds(0, 5 * chunk)], fw_r)

    @pl.when(core == 1)
    def _():
        arrived(sizes.at[pl.ds(0, 2 * chunk)], fw_r)

    root = math.sqrt(2.0 / math.pi)
    parts = 4

    def finish(i, carry):
        size = cells // parts
        rows = pl.ds(pl.multiple_of(i * size, size), size)
        lhs = brot[rows, :]
        for xp in range(cx // 2):
            rhs = coef[:, :, :, xp * 256 : xp * 256 + 256].reshape(2 * MY * MZ, 256)
            acc = jnp.dot(lhs, rhs, preferred_element_type=F32)
            for x in range(2):
                v = acc[:, x * 128 : x * 128 + 128] + conv[2 * xp + x, rows, :]
                t = jnp.tanh(v * (2.0 * root + (8.0 * 0.044715 * root) * (v * v)))
                out[2 * xp + x, rows, :] = (v + v * t).astype(BF)
        return carry

    lax.fori_loop(0, parts, finish, 0, unroll=True)

    def all_sent(count):
        ref = sizes.at[pl.ds(0, count)]
        pltpu.make_async_remote_copy(
            src_ref=ref, dst_ref=ref, send_sem=sent, recv_sem=fw_r, **peer(gx, gy)
        ).wait_send()

    pl.when(core == 0)(lambda: all_sent(sizes.shape[0] - 4 * chunk))
    pl.when(core == 1)(lambda: all_sent(sizes.shape[0]))
    for n in range(8):
        @pl.when(inside_grid(n, 1))
        def _(n=n):
            halo(n).wait_send()


def body(consts, nx, ny, flow_field, spectral_weight, conv_weight, channel_bias):
    cells_x, cells_y, cells_z, channels = flow_field.shape
    cells = cells_y * cells_z
    nz = ny // 2
    modes = 2 * MY * MZ
    v = pltpu.VMEM
    dma = pltpu.SemaphoreType.DMA
    vmem = pl.BlockSpec(memory_space=pltpu.VMEM)
    band = 64 * cells_x // 4
    sent_kib = band * (nz + (nz - 1) + 9) + 3 * (nx - 1)
    out = pl.pallas_call(
        functools.partial(kernel, nx, ny),
        out_shape=pltpu.VMEM((cells_x, cells, channels), BF),
        in_specs=[ANY] * 7,
        out_specs=vmem,
        scratch_shapes=[
            v((cells_x + 2, cells_y + 2, cells_z, channels), BF),
            v((MX, 128, 128), BF),
            v((27, 128, 128), BF),
            v((1, channels), F32),
            v((modes, cells), BF),
            v((cells, modes), BF),
            v((2 * nx * cells_x + 4 * MX, 2 * MX), BF),
            v((cells, modes), BF),
            v((modes // 2, cells_x * 128), BF),
            v((modes // 2, cells_x * 128), F32),
            v((modes // 2, cells_x * 128), BF),
            v((modes // 2, cells_x * 128), BF),
            v((nz - 1, 64, cells_x * 128), BF),
            v((256, 128), F32),
            v((nx, 4, 128), BF),
            v((nx, 4, 128), BF),
            v((nx, 8, 128), BF),
            v((nx, 8, 128), BF),
            v((2, ny, 32, cells_x * 128), BF),
            v((cells_x, cells, 128), F32),
            v((sent_kib, 4, 128), BF),
            dma((6,)),
            pltpu.SemaphoreType.REGULAR((2,)),
            dma,
            dma((8,)),
            dma((8,)),
            dma((2,)),
            dma,
            dma((2,)),
            dma((nz,)),
            dma,
            dma,
        ],
        compiler_params=pltpu.CompilerParams(collective_id=0, has_side_effects=True),
        name="layer",
    )(
        flow_field,
        spectral_weight.reshape(MX, 128, 128),
        conv_weight.reshape(27, 128, 128),
        channel_bias.reshape(1, channels),
        *consts,
    )
    return out.reshape(cells_x, cells_y, cells_z, channels)


def solution(mesh):
    nx, ny = mesh.shape["gx"], mesh.shape["gy"]
    consts = tables(nx, ny, 4, 16, 64)

    def layer(*args):
        return body(tuple(jnp.asarray(c) for c in consts), nx, ny, *args)

    placed = (P("gx", "gy", None, None), P(("gy", "gx"), None, None, None, None), P(), P())
    return jax.shard_map(
        layer, mesh=mesh, in_specs=placed, out_specs=P("gx", "gy", None, None), check_vma=False
    )
```
